128 devices in a mesh: tok: 32 (over y, x, core), kv: 4 (over z).
Axes of the slice: x: 4, y: 4, z: 4, core: 2. Of those that a mesh axis runs over, the one named last changes fastest.
Arguments:
- queries: bfloat16 [8192, 8192], P('tok', 'kv'), may hold values from -12 to 12
- key_states: bfloat16 [8192, 1024], P('tok', 'kv'), may hold values from -12 to 12
- value_states: bfloat16 [8192, 1024], P('tok', 'kv'), may hold values from -6 to 6
- doc_lengths: int32 [16], replicated, may hold values from 1 to 4096, 8192 in all
- block_plan: int32 [32, 32], replicated, may hold values from 0 to 31, each once within a row
Outputs:
- attention_out: bfloat16 [8192, 8192], P(('tok', 'kv'))
- served_lse: float32 [64, 8192], P('kv', 'tok')
The draws below stay inside these ranges and needn't reach their ends.
Inputs may be any that keep to these rules, and one draw needn't show every extreme that they name: `doc_lengths`: positive lengths that sum to 8192; the largest is exactly 4096. Every row of block_plan is a permutation of 0 to 31.
All inputs are finite; a program needn't handle non-finite values.
Results may differ from the reference program's by a relative error of at most 0.012.
The reference program's roundings to bfloat16 on the way (of `q_rot`, `k_rot` and `probs`) count: a program that leaves them out, or rounds other values in their place, can miss the bound.
Values may be sent and summed in bfloat16 or wider, within the bound.
A program may use at most 64 MiB of HBM per device.

```python
import math
import jax
import jax.numpy as jnp
import numpy as np
from jax import lax

HEAD_DIM = 128
Q_HEADS = 64
KV_HEADS = 8
TOK_DEV = 256
DOCS = 16
TOKENS = 8192
LONGEST = 4096
BLOCK = 8
N_TOK = 32


def spread_rows(key, salt, heads):
    row_key = jax.random.fold_in(key, salt)
    scales = jnp.exp(jax.random.uniform(jax.random.fold_in(row_key, 11), (TOKENS, heads, 1), jnp.float32, math.log(0.3), math.log(3.0)))
    noise = jax.random.normal(jax.random.fold_in(row_key, 12), (TOKENS, heads, HEAD_DIM), jnp.float32)
    return jnp.clip(noise * scales, -12.0, 12.0)


def draw_key_states(key, part):
    drawn_draw = spread_rows(key, 301, KV_HEADS)
    return drawn_draw.reshape(TOKENS, KV_HEADS * HEAD_DIM).astype(jnp.bfloat16)


def draw_queries(key, part):
    drawn_draw = spread_rows(key, 302, Q_HEADS)
    return drawn_draw.reshape(TOKENS, Q_HEADS * HEAD_DIM).astype(jnp.bfloat16)


def block_scale(stream_key, extent, split, low, high):
    def one(position, shards_of):
        draws = jax.random.uniform(jax.random.fold_in(jax.random.fold_in(stream_key, 6), position), (shards_of,), jnp.float32, low / len(split), high / len(split))
        return jnp.repeat(jnp.exp(draws), extent[position] // shards_of).reshape((-1,) + (1,) * (len(extent) - position - 1))

    loudness = one(*split[0])
    for cut in split[1:]:
        loudness = loudness * one(*cut)
    return loudness


def profile(count, total, limit, slope):
    portions = [(1 << 20) // math.isqrt(grade ** slope) + 1 for grade in range(2, count + 1)]
    spare, counts = total - limit - (count - 1), [1] * (count - 1)
    while spare > 0:
        candidates = [i for i in range(count - 1) if counts[i] < limit]
        pool, left = sum([portions[i] for i in candidates]), spare
        for i in candidates:
            more = min(limit - counts[i], max(1, left * portions[i] // pool), spare)
            counts[i] = counts[i] + more
            spare = spare - more
    return np.array([limit] + counts)


def ragged_sizes(stream_key, amount, total, reach, skew):
    if amount == 2:
        one = jax.random.randint(stream_key, (), max(1, total - reach), min(reach, total - 1) + 1)
        return jnp.stack([one, total - one])
    lengths = jnp.asarray(profile(amount, total, reach, skew), jnp.int32)
    pairs = (amount - 1) // 2
    giver, sink = lengths[1:1 + 2 * pairs:2], lengths[2:2 + 2 * pairs:2]
    margin = jnp.minimum(giver - 1, reach - sink)
    shifted = jax.random.randint(jax.random.fold_in(stream_key, 1), (pairs,), 0, 1 << 20) % (margin + 1)
    lengths = lengths.at[1:1 + 2 * pairs:2].set(giver - shifted).at[2:2 + 2 * pairs:2].set(sink + shifted)
    return lengths[jax.random.permutation(jax.random.fold_in(stream_key, 2), amount)]


def scatter_about(rng, shape, width, most, pieces=(), kind=jnp.bfloat16):
    drawn = width * jax.random.normal(rng, shape, jnp.float32)
    if pieces:
        drawn = drawn * block_scale(rng, shape, pieces, -0.22, 0.18)
    return jnp.clip(drawn, -most, most).astype(kind)


def setup_inputs(seed: int = 0) -> dict:
    streams_of = jax.random.split(jax.random.key(seed), 6)
    return {
        "queries": draw_queries(jax.random.fold_in(streams_of[5], 71), 0),
        "key_states": draw_key_states(jax.random.fold_in(streams_of[5], 71), 0),
        "value_states": scatter_about(streams_of[2], (TOKENS, KV_HEADS * HEAD_DIM), 1.0, 6.0, ((0, 32), (1, 4))),
        "doc_lengths": ragged_sizes(streams_of[3], DOCS, TOKENS, LONGEST, 2).astype(jnp.int32),
        "block_plan": jax.vmap(lambda own: jax.random.permutation(own, N_TOK))(jax.random.split(streams_of[4], N_TOK)).reshape((N_TOK, N_TOK)).astype(jnp.int32),
    }


THETA = 500000.0

def doc_layout(doc_lengths, token_index):
    doc_ends = jnp.cumsum(doc_lengths).astype(jnp.int32)
    passed = token_index[:, None] >= doc_ends[None, :]
    doc_ids = lax.optimization_barrier(jnp.sum(passed.astype(jnp.int32), axis=1)).astype(jnp.int32)
    starts = lax.optimization_barrier(jnp.sum(jnp.where(passed, doc_lengths[None, :], 0), axis=1)).astype(jnp.int32)
    return (doc_ids, (token_index - starts).astype(jnp.int32))

def rotate(inputs, positions, heads):
    half_dim = HEAD_DIM // 2
    inv_freq = jnp.power(jnp.float32(THETA), -(jnp.arange(half_dim, dtype=jnp.float32) * 2.0 / HEAD_DIM))
    angles = positions.astype(jnp.float32)[:, None] * inv_freq[None, :]
    cosine = jnp.cos(angles)[:, None, :]
    sine_val = jnp.sin(angles)[:, None, :]
    shaped = inputs.astype(jnp.float32).reshape(inputs.shape[0], heads, HEAD_DIM)
    leading = shaped[..., :half_dim]
    trailing = shaped[..., half_dim:]
    turned = jnp.concatenate([leading * cosine - trailing * sine_val, trailing * cosine + leading * sine_val], axis=-1)
    return turned.reshape(inputs.shape[0], heads * HEAD_DIM).astype(jnp.bfloat16)

def reference(queries, key_states, value_states, doc_lengths, block_plan):
    token_index = jnp.arange(TOKENS, dtype=jnp.int32)
    doc_ids, positions = doc_layout(doc_lengths, token_index)
    q_rot = rotate(queries, positions, Q_HEADS)
    k_rot = rotate(key_states, positions, KV_HEADS)
    per_group = Q_HEADS // KV_HEADS
    key_span = (N_TOK // 2 + 1) * TOK_DEV
    score_scale = 1.0 / math.sqrt(HEAD_DIM)

    def one_block(block_id):
        offset = (block_id * TOK_DEV).astype(jnp.int32)
        key_start = jnp.maximum(offset - N_TOK // 2 * TOK_DEV, 0).astype(jnp.int32)
        query_block = lax.dynamic_slice_in_dim(q_rot, offset, TOK_DEV, 0).astype(jnp.float32).reshape(TOK_DEV, KV_HEADS, per_group, HEAD_DIM)
        key_block = lax.dynamic_slice_in_dim(k_rot, key_start, key_span, 0).astype(jnp.float32).reshape(key_span, KV_HEADS, HEAD_DIM)
        value_block = lax.dynamic_slice_in_dim(value_states, key_start, key_span, 0).astype(jnp.float32).reshape(key_span, KV_HEADS, HEAD_DIM)
        scores = jnp.einsum('rgqd,ngd->gqrn', query_block, key_block) * score_scale
        query_index = offset + jnp.arange(TOK_DEV, dtype=jnp.int32)
        key_index = key_start + jnp.arange(key_span, dtype=jnp.int32)
        query_docs = lax.dynamic_slice_in_dim(doc_ids, offset, TOK_DEV, 0)
        key_docs = lax.dynamic_slice_in_dim(doc_ids, key_start, key_span, 0)
        allowed = (query_docs[:, None] == key_docs[None, :]) & (key_index[None, :] <= query_index[:, None])
        scores = jnp.where(allowed, scores, -jnp.inf)
        row_max = lax.optimization_barrier(jnp.max(scores, axis=-1))
        weights = jnp.exp(scores - row_max[..., None])
        row_sum = lax.optimization_barrier(jnp.sum(weights, axis=-1))
        probs = lax.optimization_barrier(weights.astype(jnp.bfloat16)).astype(jnp.float32)
        mixed = jnp.einsum('gqrn,ngd->rgqd', probs, value_block)
        mixed = mixed / jnp.transpose(row_sum, (2, 0, 1))[..., None]
        log_norm = (row_max + jnp.log(row_sum)).reshape(Q_HEADS, TOK_DEV)
        return (mixed.reshape(TOK_DEV, Q_HEADS * HEAD_DIM).astype(jnp.bfloat16), log_norm)
    outputs, norms = lax.map(one_block, jnp.arange(N_TOK, dtype=jnp.int32))
    attention_out = outputs.reshape(TOKENS, Q_HEADS * HEAD_DIM)
    log_all = jnp.transpose(norms, (1, 0, 2)).reshape(Q_HEADS, TOKENS)
    served_order = (jnp.arange(N_TOK, dtype=jnp.int32)[None, :, None] * TOK_DEV + jnp.transpose(block_plan)[:, :, None] * BLOCK + jnp.arange(BLOCK, dtype=jnp.int32)[None, None, :]).reshape(TOKENS).astype(jnp.int32)
    served_lse = jnp.take(log_all, served_order, axis=1)
    return (attention_out, served_lse)
```

```python
import functools
import math

import jax
import jax.numpy as jnp
import numpy as np
from jax import lax
from jax.experimental import pallas as pl
from jax.experimental.pallas import tpu as pltpu
from jax.sharding import PartitionSpec as P

D = 128
T = 256
GROUPS = 2
PER = 8
N_TOK = 32
N_KV = 4
DOCS = 16
BACK = 16
SLOTS = 24
NEG = -1e30
THETA = 500000.0
SCALE = 1.0 / math.sqrt(D)
C2 = SCALE * math.log2(math.e)
MESH = pl.DeviceIdType.MESH
BF = jnp.bfloat16
F32 = jnp.float32


def kernel(
    doc_ref, freq_ref, plan_ref, q_ref, k_ref, v_ref,
    out_ref, lse_ref,
    kv, qrot, scores, peak, obuf, start_ref, cos_ref, sin_ref, lse_own, lse_send, lse_recv,
    ksend, krecv, osend, orecv, lsend, lrecv,
):
    j = lax.axis_index("tok")
    z = lax.axis_index("kv")
    core = j % 2
    x = (j // 2) % 4
    y = j // 8
    pos = j % 8

    def tok_of(y_, x_, core_):
        return ((y_ % 4) * 4 + (x_ % 4)) * 2 + core_

    up = tok_of(y + 1, x, core)
    right = tok_of(y, x + 1, core)
    left = tok_of(y, x + 3, core)
    twin = tok_of(y, x, 1 - core)
    pos_r = (pos + 2) % 8
    pos_l = (pos + 6) % 8
    pos_f = (pos + 4) % 8

    barrier = pltpu.get_barrier_semaphore()

    def greet(d, _):
        pl.semaphore_signal(
            barrier, inc=1, device_id={"tok": (j + d) % N_TOK}, device_id_type=MESH
        )
        return 0

    lax.fori_loop(1, N_TOK, greet, 0)
    for d in range(1, N_KV):
        pl.semaphore_signal(
            barrier, inc=1, device_id={"kv": (z + d) % N_KV}, device_id_type=MESH
        )

    token = j * T + lax.broadcasted_iota(jnp.int32, (T, D), 0)
    lane = lax.broadcasted_iota(jnp.int32, (T, D), 1)
    start = jnp.zeros((T, D), jnp.int32)
    end = jnp.int32(0)
    for i in range(DOCS):
        end = end + doc_ref[i]
        start = jnp.where(token >= end, end, start)
    start_ref[...] = start - (j - BACK) * T
    angle = (token - start).astype(F32) * freq_ref[...]
    cos_ref[...] = jnp.cos(angle)
    sine = jnp.sin(angle)
    sin_ref[...] = jnp.where(lane < D // 2, -sine, sine)

    def rotate(block):
        wide = block.astype(F32)
        return (wide * cos_ref[...] + pltpu.roll(wide, D // 2, 1) * sin_ref[...]).astype(BF)

    for g in range(GROUPS):
        kv[2 * g, 16 + pos] = rotate(k_ref[:, g * D : (g + 1) * D])
        kv[2 * g + 1, 16 + pos] = v_ref[:, g * D : (g + 1) * D]

    pl.semaphore_wait(barrier, N_TOK - 1 + N_KV - 1)

    def copy(t, slot, n, to):
        return pltpu.make_async_remote_copy(
            src_ref=kv.at[t, slot],
            dst_ref=kv.at[t, slot],
            send_sem=ksend.at[t, n],
            recv_sem=krecv.at[t, slot],
            device_id={"tok": to},
            device_id_type=MESH,
        )

    def copy_up(t, row, n):
        return pltpu.make_async_remote_copy(
            src_ref=kv.at[t, row * 8 + pos],
            dst_ref=kv.at[t, (row - 1) * 8 + pos],
            send_sem=ksend.at[t, n],
            recv_sem=krecv.at[t, (row - 1) * 8 + pos],
            device_id={"tok": up},
            device_id_type=MESH,
        )

    def spread(t, row):
        n = row * 7
        copy(t, row * 8 + pos, n, right).start()
        copy(t, row * 8 + pos, n + 1, left).start()
        copy(t, row * 8 + pos, n + 2, twin).start()

    def pass_on(t, row):
        n = row * 7
        copy(t, row * 8 + pos_l, n + 3, right).wait_recv()
        copy(t, row * 8 + pos_r, n + 3, right).wait_recv()
        far_from = jnp.where(t % 2 == 0, pos_l, pos_r)
        far_to = jnp.where(t % 2 == 0, right, left)
        copy(t, row * 8 + far_from, n + 3, far_to).start()
        copy(t, row * 8 + pos_l, n + 4, twin).start()
        copy(t, row * 8 + pos_r, n + 5, twin).start()

    def last_on(t, row):
        copy(t, row * 8 + pos_f, row * 7 + 6, twin).wait_recv()
        copy(t, row * 8 + pos_f, row * 7 + 6, twin).start()

    def gather(t, _):
        copy_up(t, 2, 21).start()
        spread(t, 2)
        copy(t, 8 + pos, 0, up).wait_recv()
        copy_up(t, 1, 22).start()
        spread(t, 1)
        pass_on(t, 2)
        copy(t, pos, 0, up).wait_recv()
        spread(t, 0)
        pass_on(t, 1)
        last_on(t, 2)
        pass_on(t, 0)
        last_on(t, 1)
        last_on(t, 0)
        return 0

    def settle(t, _):
        def one(i, _):
            slot = (i // 4) * 8 + (i % 4) * 2 + 1 - core
            copy(t, slot, 0, twin).wait_recv()
            return 0

        lax.fori_loop(0, 12, one, 0)
        return 0

    def drain(t, _):
        def one(n, _):
            copy(t, 0, n, twin).wait_send()
            return 0

        lax.fori_loop(0, 23, one, 0)
        return 0

    for h in range(GROUPS * PER):
        qrot[h] = rotate(q_ref[:, h * D : (h + 1) * D])

    lax.fori_loop(0, 4, gather, 0)
    lax.fori_loop(0, 4, settle, 0)

    column = lax.broadcasted_iota(jnp.int32, (8, D), 1)

    def score(g, h, keys):
        return lax.dot_general(
            qrot[g * PER + h], keys, (((1,), (1,)), ((), ())), preferred_element_type=F32
        )

    def pass1(g):
        def pair(i, first):
            keys = jnp.concatenate([kv[2 * g, pos + 2 * i], kv[2 * g, pos + 2 * i + 1]], axis=0)

            def head(h, _):
                s = score(g, h, keys)
                best = peak[h]
                for c in range(4):
                    index = column + (i * 512 + c * D)
                    allowed = index[None] >= start_ref[...].reshape(T // 8, 8, D)
                    part = jnp.where(allowed.reshape(T, D), s[:, c * D : (c + 1) * D], NEG)
                    scores[i * 2 + c // 2, h, :, (c % 2) * D : (c % 2 + 1) * D] = part
                    best = jnp.maximum(best, part)
                peak[h] = best
                return 0

            lax.fori_loop(0, PER, head, 0, unroll=True)
            return first

        keys = kv[2 * g, pos + BACK]

        def diagonal(h, _):
            s = score(g, h, keys)
            row = lax.broadcasted_iota(jnp.int32, (T, D), 0)
            best = jnp.full((T, D), NEG, F32)
            for c in range(2):
                index = lax.broadcasted_iota(jnp.int32, (T, D), 1) + c * D
                allowed = (index + BACK * T >= start_ref[...]) & (index <= row)
                part = jnp.where(allowed, s[:, c * D : (c + 1) * D], NEG)
                scores[BACK, h, :, c * D : (c + 1) * D] = part
                best = jnp.maximum(best, part)
            peak[h] = best
            return 0

        lax.fori_loop(0, PER, diagonal, 0, unroll=True)
        lax.fori_loop(0, BACK // 2, pair, 0)

    def out_copy(head, d):
        to = (z + d) % N_KV
        return pltpu.make_async_remote_copy(
            src_ref=obuf.at[head, pl.ds(to * 64, 64), :],
            dst_ref=out_ref.at[:, pl.ds(pl.multiple_of((z * 16 + head) * D, D), D)],
            send_sem=osend.at[head, d],
            recv_sem=orecv.at[head, d],
            device_id={"kv": to},
            device_id_type=MESH,
        )

    def pass2(g):
        values = jnp.concatenate([kv[2 * g + 1, pos + i] for i in range(BACK + 1)], axis=0)

        def head(h, _):
            top = jnp.max(peak[h], axis=1, keepdims=True)
            wide = jnp.broadcast_to(top, (T, D))
            total = jnp.zeros((T, D), F32)
            probs = []
            for i in range(BACK + 1):
                for c in range(2):
                    p = jnp.exp2((scores[i, h, :, c * D : (c + 1) * D] - wide) * C2)
                    total = total + p
                    probs.append(p.astype(BF))
            mixed = jnp.dot(
                jnp.concatenate(probs, axis=1), values, preferred_element_type=F32
            )
            row_sum = jnp.sum(total, axis=1, keepdims=True)
            here = g * PER + h
            obuf[here] = (mixed / row_sum).astype(BF)
            norm = top * SCALE + jnp.log(row_sum)
            lse_own[...] = jnp.where(lane == here, norm, lse_own[...])
            for d in range(1, N_KV):
                out_copy(here, d).start()
            out_ref[:, pl.ds(pl.multiple_of((z * 16 + here) * D, D), D)] = obuf[
                here, pl.ds(pl.multiple_of(z * 64, 64), 64), :
            ]
            return 0

        lax.fori_loop(0, PER, head, 0)

    lse_own[...] = jnp.zeros((T, D), F32)
    for g in range(GROUPS):
        pass1(g)
        pass2(g)

    spread_rows = (
        lax.broadcasted_iota(jnp.int32, (T, N_TOK), 0) // 8
        == lax.broadcasted_iota(jnp.int32, (T, N_TOK), 1)
    ).astype(F32)
    plans = lax.dot_general(
        spread_rows.astype(BF), plan_ref[...].astype(F32).astype(BF),
        (((1,), (1,)), ((), ())), preferred_element_type=F32,
    )
    mine = lax.broadcasted_iota(jnp.int32, (T, N_TOK), 1) == j
    block = jnp.sum(jnp.where(mine, plans, 0.0), axis=1, keepdims=True).astype(jnp.int32)
    wanted = block * 8 + lax.broadcasted_iota(jnp.int32, (T, T), 0) % 8
    pick = (wanted == lax.broadcasted_iota(jnp.int32, (T, T), 1)).astype(F32).astype(BF)
    rest = lse_own[...]
    ordered = jnp.zeros((T, D), F32)
    for _ in range(3):
        piece = rest.astype(BF)
        rest = rest - piece.astype(F32)
        ordered = ordered + jnp.dot(pick, piece, preferred_element_type=F32)
    lse_send[...] = ordered.reshape(N_TOK, 8, D)
    lse_recv[j] = lse_send[j]

    def lse_copy(d):
        to = (j + d) % N_TOK
        return pltpu.make_async_remote_copy(
            src_ref=lse_send.at[to],
            dst_ref=lse_recv.at[j],
            send_sem=lsend.at[d],
            recv_sem=lrecv.at[d],
            device_id={"tok": to},
            device_id_type=MESH,
        )

    def lse_start(d, _):
        lse_copy(d).start()
        return 0

    def lse_wait(d, _):
        lse_copy(d).wait()
        return 0

    lax.fori_loop(1, N_TOK, lse_start, 0)
    lax.fori_loop(0, 4, drain, 0)
    lax.fori_loop(1, N_TOK, lse_wait, 0)
    lse_ref[...] = lse_recv[...].reshape(T, D).T[:16, :]

    def out_wait(h, _):
        for d in range(1, N_KV):
            out_copy(h, d).wait()
        return 0

    lax.fori_loop(0, GROUPS * PER, out_wait, 0)


def body(queries, key_states, value_states, doc_lengths, block_plan):
    half = np.power(THETA, -(np.arange(D // 2) * 2.0 / D)).astype(np.float32)
    freq = jnp.asarray(np.concatenate([half, half])[None, :])
    vmem = pl.BlockSpec(memory_space=pltpu.VMEM)
    return pl.pallas_call(
        kernel,
        out_shape=(
            jax.ShapeDtypeStruct((T // N_KV, N_KV * GROUPS * PER * D), BF),
            jax.ShapeDtypeStruct((GROUPS * PER, T), F32),
        ),
        in_specs=[pl.BlockSpec(memory_space=pltpu.SMEM)] + [vmem] * 5,
        out_specs=(vmem, vmem),
        scratch_shapes=[
            pltpu.VMEM((4, SLOTS, T, D), BF),
            pltpu.VMEM((GROUPS * PER, T, D), BF),
            pltpu.VMEM((BACK + 1, PER, T, T), F32),
            pltpu.VMEM((PER, T, D), F32),
            pltpu.VMEM((GROUPS * PER, T, D), BF),
            pltpu.VMEM((T, D), jnp.int32),
            pltpu.VMEM((T, D), F32),
            pltpu.VMEM((T, D), F32),
            pltpu.VMEM((T, D), F32),
            pltpu.VMEM((N_TOK, 8, D), F32),
            pltpu.VMEM((N_TOK, 8, D), F32),
            pltpu.SemaphoreType.DMA((4, 23)),
            pltpu.SemaphoreType.DMA((4, SLOTS)),
            pltpu.SemaphoreType.DMA((GROUPS * PER, N_KV)),
            pltpu.SemaphoreType.DMA((GROUPS * PER, N_KV)),
            pltpu.SemaphoreType.DMA((N_TOK,)),
            pltpu.SemaphoreType.DMA((N_TOK,)),
        ],
        compiler_params=pltpu.CompilerParams(
            collective_id=0, has_side_effects=True, vmem_limit_bytes=60 << 20
        ),
    )(doc_lengths, freq, block_plan, queries, key_states, value_states)


def solution(mesh):
    return jax.shard_map(
        body,
        mesh=mesh,
        in_specs=(P("tok", "kv"), P("tok", "kv"), P("tok", "kv"), P(), P()),
        out_specs=(P(("tok", "kv"), None), P("kv", "tok")),
        check_vma=False,
    )
```

```python
import functools
import math

import jax
import jax.numpy as jnp
import numpy as np
from jax import lax
from jax.experimental import pallas as pl
from jax.experimental.pallas import tpu as pltpu
from jax.sharding import PartitionSpec as P

D = 128
T = 256
GROUPS = 2
PER = 8
N_TOK = 32
N_KV = 4
DOCS = 16
BACK = 16
SLOTS = 24
NEG = -1e30
THETA = 500000.0
SCALE = 1.0 / math.sqrt(D)
C2 = SCALE * math.log2(math.e)
MESH = pl.DeviceIdType.MESH
BF = jnp.bfloat16
F32 = jnp.float32


def kernel(
    doc_ref, freq_ref, plan_ref, q_ref, k_ref, v_ref,
    out_ref, lse_ref,
    kv, qrot, scores, peak, obuf, start_ref, cos_ref, sin_ref, lse_own, lse_send, lse_recv,
    ksend, krecv, osend, orecv, lsend, lrecv,
):
    j = lax.axis_index("tok")
    z = lax.axis_index("kv")
    core = j % 2
    x = (j // 2) % 4
    y = j // 8
    pos = j % 8

    def tok_of(y_, x_, core_):
        return ((y_ % 4) * 4 + (x_ % 4)) * 2 + core_

    up = tok_of(y + 1, x, core)
    right = tok_of(y, x + 1, core)
    left = tok_of(y, x + 3, core)
    twin = tok_of(y, x, 1 - core)
    pos_r = (pos + 2) % 8
    pos_l = (pos + 6) % 8
    pos_f = (pos + 4) % 8

    barrier = pltpu.get_barrier_semaphore()

    def greet(d, _):
        pl.semaphore_signal(
            barrier, inc=1, device_id={"tok": (j + d) % N_TOK}, device_id_type=MESH
        )
        return 0

    lax.fori_loop(1, N_TOK, greet, 0)
    for d in range(1, N_KV):
        pl.semaphore_signal(
            barrier, inc=1, device_id={"kv": (z + d) % N_KV}, device_id_type=MESH
        )

    token = j * T + lax.broadcasted_iota(jnp.int32, (T, D), 0)
    lane = lax.broadcasted_iota(jnp.int32, (T, D), 1)
    start = jnp.zeros((T, D), jnp.int32)
    end = jnp.int32(0)
    for i in range(DOCS):
        end = end + doc_ref[i]
        start = jnp.where(token >= end, end, start)
    start_ref[...] = start - (j - BACK) * T
    angle = (token - start).astype(F32) * freq_ref[...]
    cos_ref[...] = jnp.cos(angle)
    sine = jnp.sin(angle)
    sin_ref[...] = jnp.where(lane < D // 2, -sine, sine)

    def rotate(block):
        wide = block.astype(F32)
        return (wide * cos_ref[...] + pltpu.roll(wide, D // 2, 1) * sin_ref[...]).astype(BF)

    for g in range(GROUPS):
        kv[2 * g, 16 + pos] = rotate(k_ref[:, g * D : (g + 1) * D])
        kv[2 * g + 1, 16 + pos] = v_ref[:, g * D : (g + 1) * D]

    pl.semaphore_wait(barrier, N_TOK - 1 + N_KV - 1)

    def copy(t, slot, n, to):
        return pltpu.make_async_remote_copy(
            src_ref=kv.at[t, slot],
            dst_ref=kv.at[t, slot],
            send_sem=ksend.at[t, n],
            recv_sem=krecv.at[t, slot],
            device_id={"tok": to},
            device_id_type=MESH,
        )

    def copy_up(t, row, n):
        return pltpu.make_async_remote_copy(
            src_ref=kv.at[t, row * 8 + pos],
            dst_ref=kv.at[t, (row - 1) * 8 + pos],
            send_sem=ksend.at[t, n],
            recv_sem=krecv.at[t, (row - 1) * 8 + pos],
            device_id={"tok": up},
            device_id_type=MESH,
        )

    def spread(t, row):
        n = row * 7
        copy(t, row * 8 + pos, n, right).start()
        copy(t, row * 8 + pos, n + 1, left).start()
        copy(t, row * 8 + pos, n + 2, twin).start()

    def pass_on(t, row):
        n = row * 7
        copy(t, row * 8 + pos_l, n + 3, right).wait_recv()
        copy(t, row * 8 + pos_r, n + 3, right).wait_recv()
        far_from = jnp.where(t % 2 == 0, pos_l, pos_r)
        far_to = jnp.where(t % 2 == 0, right, left)
        copy(t, row * 8 + far_from, n + 3, far_to).start()
        copy(t, row * 8 + pos_l, n + 4, twin).start()
        copy(t, row * 8 + pos_r, n + 5, twin).start()

    def last_on(t, row):
        copy(t, row * 8 + pos_f, row * 7 + 6, twin).wait_recv()
        copy(t, row * 8 + pos_f, row * 7 + 6, twin).start()

    def stage_a(t):
        copy_up(t, 2, 21).start()
        spread(t, 2)

    def stage_b(t):
        copy(t, 8 + pos, 0, up).wait_recv()
        copy_up(t, 1, 22).start()
        spread(t, 1)

    def stage_d(t):
        copy(t, pos, 0, up).wait_recv()
        spread(t, 0)

    def settle(t, row):
        def one(i, _):
            copy(t, row * 8 + i * 2 + 1 - core, 0, twin).wait_recv()
            return 0

        lax.fori_loop(0, 4, one, 0)

    def drain(t, _):
        def one(n, _):
            copy(t, 0, n, twin).wait_send()
            return 0

        lax.fori_loop(0, 23, one, 0)
        return 0

    def turn(h, _):
        lanes = pl.ds(pl.multiple_of(h * D, D), D)
        qrot[h] = rotate(q_ref[:, lanes])
        return 0

    stage_a(0)
    lax.fori_loop(0, PER, turn, 0)
    stage_b(0)
    pass_on(0, 2)
    stage_d(0)
    pass_on(0, 1)
    last_on(0, 2)
    stage_a(1)
    lax.fori_loop(PER, 2 * PER, turn, 0)
    last_on(0, 1)
    pass_on(0, 0)
    settle(0, 2)
    settle(0, 1)
    stage_b(1)

    column = lax.broadcasted_iota(jnp.int32, (8, D), 1)

    def score(g, h, keys):
        return lax.dot_general(
            qrot[g * PER + h], keys, (((1,), (1,)), ((), ())), preferred_element_type=F32
        )

    def pass1(g, hooks):
        def pair(k, _):
            hooks(k)
            i = BACK // 2 - 1 - k
            keys = jnp.concatenate([kv[2 * g, pos + 2 * i], kv[2 * g, pos + 2 * i + 1]], axis=0)

            def head(h, _):
                s = score(g, h, keys)
                best = peak[h]
                for c in range(4):
                    index = column + (i * 512 + c * D)
                    allowed = index[None] >= start_ref[...].reshape(T // 8, 8, D)
                    part = jnp.where(allowed.reshape(T, D), s[:, c * D : (c + 1) * D], NEG)
                    scores[i * 2 + c // 2, h, :, (c % 2) * D : (c % 2 + 1) * D] = part
                    best = jnp.maximum(best, part)
                peak[h] = best
                return 0

            lax.fori_loop(0, PER, head, 0, unroll=True)
            return 0

        keys = kv[2 * g, pos + BACK]

        def diagonal(h, _):
            s = score(g, h, keys)
            row = lax.broadcasted_iota(jnp.int32, (T, D), 0)
            best = jnp.full((T, D), NEG, F32)
            for c in range(2):
                index = lax.broadcasted_iota(jnp.int32, (T, D), 1) + c * D
                allowed = (index + BACK * T >= start_ref[...]) & (index <= row)
                part = jnp.where(allowed, s[:, c * D : (c + 1) * D], NEG)
                scores[BACK, h, :, c * D : (c + 1) * D] = part
                best = jnp.maximum(best, part)
            peak[h] = best
            return 0

        lax.fori_loop(0, PER, diagonal, 0, unroll=True)
        lax.fori_loop(0, BACK // 2, pair, 0)

    def out_copy(head, d):
        to = (z + d) % N_KV
        return pltpu.make_async_remote_copy(
            src_ref=obuf.at[head, pl.ds(to * 64, 64), :],
            dst_ref=out_ref.at[:, pl.ds(pl.multiple_of((z * 16 + head) * D, D), D)],
            send_sem=osend.at[head, d],
            recv_sem=orecv.at[head, d],
            device_id={"kv": to},
            device_id_type=MESH,
        )

    def pass2(g, hooks):
        values = jnp.concatenate([kv[2 * g + 1, pos + i] for i in range(BACK + 1)], axis=0)

        def head(h, _):
            hooks(h)
            top = jnp.max(peak[h], axis=1, keepdims=True)
            wide = jnp.broadcast_to(top, (T, D))
            total = jnp.zeros((T, D), F32)
            probs = []
            for i in range(BACK + 1):
                for c in range(2):
                    p = jnp.exp2((scores[i, h, :, c * D : (c + 1) * D] - wide) * C2)
                    total = total + p
                    probs.append(p.astype(BF))
            mixed = jnp.dot(
                jnp.concatenate(probs, axis=1), values, preferred_element_type=F32
            )
            row_sum = jnp.sum(total, axis=1, keepdims=True)
            here = g * PER + h
            obuf[here] = (mixed / row_sum).astype(BF)
            norm = top * SCALE + jnp.log(row_sum)
            lse_own[...] = jnp.where(lane == here, norm, lse_own[...])
            for d in range(1, N_KV):
                out_copy(here, d).start()
            out_ref[:, pl.ds(pl.multiple_of((z * 16 + here) * D, D), D)] = obuf[
                here, pl.ds(pl.multiple_of(z * 64, 64), 64), :
            ]
            return 0

        lax.fori_loop(0, PER, head, 0)

    lse_own[...] = jnp.zeros((T, D), F32)
    def hooks_of(table):
        def hooks(k):
            for step, calls in table.items():

                @pl.when(k == step)
                def _():
                    for call, *where in calls:
                        call(*where)

        return hooks

    pass1(0, hooks_of({
        0: [(pass_on, 1, 2)],
        1: [(last_on, 0, 0), (stage_d, 1)],
        2: [(pass_on, 1, 1), (last_on, 1, 2)],
        4: [(settle, 0, 0), (pass_on, 1, 0)],
        5: [(last_on, 1, 1), (stage_a, 2)],
        7: [(last_on, 1, 0), (stage_b, 2)],
    }))
    for row in range(3):
        settle(1, row)
    pass2(0, hooks_of({
        0: [(pass_on, 2, 2), (stage_d, 2)],
        2: [(pass_on, 2, 1), (last_on, 2, 2)],
        3: [(stage_a, 3)],
        4: [(pass_on, 2, 0), (last_on, 2, 1)],
        5: [(stage_b, 3), (pass_on, 3, 2)],
        6: [(last_on, 2, 0)],
        7: [(stage_d, 3)],
    }))
    for row in range(3):
        settle(2, row)
    pass1(1, hooks_of({
        0: [(pass_on, 3, 1), (last_on, 3, 2)],
        2: [(pass_on, 3, 0), (last_on, 3, 1)],
        4: [(last_on, 3, 0)],
    }))
    for row in range(3):
        settle(3, row)
    pass2(1, lambda h: None)

    spread_rows = (
        lax.broadcasted_iota(jnp.int32, (T, N_TOK), 0) // 8
        == lax.broadcasted_iota(jnp.int32, (T, N_TOK), 1)
    ).astype(F32)
    plans = lax.dot_general(
        spread_rows.astype(BF), plan_ref[...].astype(F32).astype(BF),
        (((1,), (1,)), ((), ())), preferred_element_type=F32,
    )
    mine = lax.broadcasted_iota(jnp.int32, (T, N_TOK), 1) == j
    block = jnp.sum(jnp.where(mine, plans, 0.0), axis=1, keepdims=True).astype(jnp.int32)
    wanted = block * 8 + lax.broadcasted_iota(jnp.int32, (T, T), 0) % 8
    pick = (wanted == lax.broadcasted_iota(jnp.int32, (T, T), 1)).astype(F32).astype(BF)
    rest = lse_own[...]
    ordered = jnp.zeros((T, D), F32)
    for _ in range(3):
        piece = rest.astype(BF)
        rest = rest - piece.astype(F32)
        ordered = ordered + jnp.dot(pick, piece, preferred_element_type=F32)
    lse_send[...] = ordered.reshape(N_TOK, 8, D)
    lse_recv[j] = lse_send[j]

    def lse_copy(d):
        to = (j + d) % N_TOK
        return pltpu.make_async_remote_copy(
            src_ref=lse_send.at[to],
            dst_ref=lse_recv.at[j],
            send_sem=lsend.at[d],
            recv_sem=lrecv.at[d],
            device_id={"tok": to},
            device_id_type=MESH,
        )

    def lse_start(d, _):
        lse_copy(d).start()
        return 0

    def lse_wait(d, _):
        lse_copy(d).wait()
        return 0

    lax.fori_loop(1, N_TOK, lse_start, 0)
    lax.fori_loop(0, 4, drain, 0)
    lax.fori_loop(1, N_TOK, lse_wait, 0)
    lse_ref[...] = lse_recv[...].reshape(T, D).T[:16, :]

    def out_wait(h, _):
        for d in range(1, N_KV):
            out_copy(h, d).wait()
        return 0

    lax.fori_loop(0, GROUPS * PER, out_wait, 0)


def body(queries, key_states, value_states, doc_lengths, block_plan):
    half = np.power(THETA, -(np.arange(D // 2) * 2.0 / D)).astype(np.float32)
    freq = jnp.asarray(np.concatenate([half, half])[None, :])
    vmem = pl.BlockSpec(memory_space=pltpu.VMEM)
    return pl.pallas_call(
        kernel,
        out_shape=(
            jax.ShapeDtypeStruct((T // N_KV, N_KV * GROUPS * PER * D), BF),
            jax.ShapeDtypeStruct((GROUPS * PER, T), F32),
        ),
        in_specs=[pl.BlockSpec(memory_space=pltpu.SMEM)] + [vmem] * 5,
        out_specs=(vmem, vmem),
        scratch_shapes=[
            pltpu.VMEM((4, SLOTS, T, D), BF),
            pltpu.VMEM((GROUPS * PER, T, D), BF),
            pltpu.VMEM((BACK + 1, PER, T, T), F32),
            pltpu.VMEM((PER, T, D), F32),
            pltpu.VMEM((GROUPS * PER, T, D), BF),
            pltpu.VMEM((T, D), jnp.int32),
            pltpu.VMEM((T, D), F32),
            pltpu.VMEM((T, D), F32),
            pltpu.VMEM((T, D), F32),
            pltpu.VMEM((N_TOK, 8, D), F32),
            pltpu.VMEM((N_TOK, 8, D), F32),
            pltpu.SemaphoreType.DMA((4, 23)),
            pltpu.SemaphoreType.DMA((4, SLOTS)),
            pltpu.SemaphoreType.DMA((GROUPS * PER, N_KV)),
            pltpu.SemaphoreType.DMA((GROUPS * PER, N_KV)),
            pltpu.SemaphoreType.DMA((N_TOK,)),
            pltpu.SemaphoreType.DMA((N_TOK,)),
        ],
        compiler_params=pltpu.CompilerParams(
            collective_id=0, has_side_effects=True, vmem_limit_bytes=60 << 20
        ),
    )(doc_lengths, freq, block_plan, queries, key_states, value_states)


def solution(mesh):
    return jax.shard_map(
        body,
        mesh=mesh,
        in_specs=(P("tok", "kv"), P("tok", "kv"), P("tok", "kv"), P(), P()),
        out_specs=(P(("tok", "kv"), None), P("kv", "tok")),
        check_vma=False,
    )
```

```python
import functools
import math

import jax
import jax.numpy as jnp
import numpy as np
from jax import lax
from jax.experimental import pallas as pl
from jax.experimental.pallas import tpu as pltpu
from jax.sharding import PartitionSpec as P

D = 128
T = 256
GROUPS = 2
PER = 8
N_TOK = 32
N_KV = 4
DOCS = 16
BACK = 16
SLOTS = 24
NEG = -1e30
THETA = 500000.0
SCALE = 1.0 / math.sqrt(D)
C2 = SCALE * math.log2(math.e)
MESH = pl.DeviceIdType.MESH
BF = jnp.bfloat16
F32 = jnp.float32


def kernel(
    doc_ref, freq_ref, plan_ref, q_hbm, k_hbm, v_hbm,
    out_ref, lse_ref,
    q_ref, k_ref, v_ref, kv, qrot, scores, peak, obuf, start_ref, cos_ref, sin_ref, lse_own, lse_send, lse_recv,
    insem, ksend, krecv, trecv, osend, orecv, lsend, lrecv,
):
    j = lax.axis_index("tok")
    z = lax.axis_index("kv")
    core = j % 2
    x = (j // 2) % 4
    y = j // 8
    pos = j % 8
    own = core * 4 + x

    loads = [
        pltpu.make_async_copy(k_hbm, k_ref, insem.at[0]),
        pltpu.make_async_copy(v_hbm, v_ref, insem.at[1]),
        pltpu.make_async_copy(q_hbm, q_ref, insem.at[2]),
    ]
    for load in loads:
        load.start()

    def tok_of(y_, x_, core_):
        return ((y_ % 4) * 4 + (x_ % 4)) * 2 + core_

    barrier = pltpu.get_barrier_semaphore()

    def greet(d, _):
        pl.semaphore_signal(
            barrier, inc=1, device_id={"tok": (j + d) % N_TOK}, device_id_type=MESH
        )
        return 0

    lax.fori_loop(1, N_TOK, greet, 0)
    for d in range(1, N_KV):
        pl.semaphore_signal(
            barrier, inc=1, device_id={"kv": (z + d) % N_KV}, device_id_type=MESH
        )

    token = j * T + lax.broadcasted_iota(jnp.int32, (T, D), 0)
    lane = lax.broadcasted_iota(jnp.int32, (T, D), 1)
    start = jnp.zeros((T, D), jnp.int32)
    end = jnp.int32(0)
    for i in range(DOCS):
        end = end + doc_ref[i]
        start = jnp.where(token >= end, end, start)
    start_ref[...] = start - (j - BACK) * T
    angle = (token - start).astype(F32) * freq_ref[...]
    cos_ref[...] = jnp.cos(angle)
    sine = jnp.sin(angle)
    sin_ref[...] = jnp.where(lane < D // 2, -sine, sine)

    def rotate(block):
        wide = block.astype(F32)
        return (wide * cos_ref[...] + pltpu.roll(wide, D // 2, 1) * sin_ref[...]).astype(BF)

    loads[0].wait()
    loads[1].wait()
    for g in range(GROUPS):
        kv[2 * g, 16 + own] = rotate(k_ref[:, g * D : (g + 1) * D])
        kv[2 * g + 1, 16 + own] = v_ref[:, g * D : (g + 1) * D]

    pl.semaphore_wait(barrier, N_TOK - 1 + N_KV - 1)

    def copy(t, source, target, to):
        return pltpu.make_async_remote_copy(
            src_ref=kv.at[t, source],
            dst_ref=kv.at[t, target],
            send_sem=ksend.at[t],
            recv_sem=krecv.at[t, target],
            device_id={"tok": to},
            device_id_type=MESH,
        )

    def share(t, row):
        mine = pl.ds(row * 8 + core * 4, 4)
        return pltpu.make_async_remote_copy(
            src_ref=kv.at[t, mine],
            dst_ref=kv.at[t, mine],
            send_sem=ksend.at[t],
            recv_sem=trecv.at[t, row],
            device_id={"tok": tok_of(y, x, 1 - core)},
            device_id_type=MESH,
        )

    def needs(row, source_x, target_x):
        return (target_x > source_x) if row == 2 else (target_x < source_x)

    def spread(t, row):
        slot = row * 8 + own
        for d in (1, 3, 2):
            target_x = (x + d) % 4

            def send():
                copy(t, slot, slot, tok_of(y, target_x, core)).start()

            if row == 1:
                send()
            else:
                pl.when(needs(row, x, target_x))(send)

    def stage_a(t):
        for d in (1, 2):
            copy(t, 16 + own, 16 - 8 * d + own, tok_of(y + d, x, core)).start()
        spread(t, 2)

    def stage_b(t):
        for row in (1, 0):
            copy(t, 0, row * 8 + own, j).wait_recv()
            spread(t, row)

    def stage_t(t, row):
        for d in (1, 3, 2):
            source_x = (x + 4 - d) % 4

            def arrive():
                copy(t, 0, row * 8 + core * 4 + source_x, j).wait_recv()

            if row == 1:
                arrive()
            else:
                pl.when(needs(row, source_x, x))(arrive)
        share(t, row).start()

    def settle(t, row):
        pltpu.make_async_copy(
            kv.at[t, pl.ds(0, 4)], kv.at[t, pl.ds(row * 8, 4)], trecv.at[t, row]
        ).wait()

    def drain(t):
        part = kv.at[t, pl.ds(0, 20)]
        pltpu.make_async_copy(part, part, ksend.at[t]).wait()

    def turn(h, _):
        lanes = pl.ds(pl.multiple_of(h * D, D), D)
        qrot[h] = rotate(q_ref[:, lanes])
        return 0

    stage_a(0)
    loads[2].wait()
    lax.fori_loop(0, PER, turn, 0)
    stage_b(0)
    stage_a(1)
    lax.fori_loop(PER, 2 * PER, turn, 0)
    stage_t(0, 2)
    stage_t(0, 1)
    stage_b(1)
    stage_t(0, 0)
    settle(0, 2)
    settle(0, 1)

    def tile(t, i):
        at = pos + i
        place = at % 8
        return kv[t, (at // 8) * 8 + (place % 2) * 4 + place // 2]

    column = lax.broadcasted_iota(jnp.int32, (8, D), 1)

    def score(g, h, keys):
        return lax.dot_general(
            qrot[g * PER + h], keys, (((1,), (1,)), ((), ())), preferred_element_type=F32
        )

    def pass1(g, hooks):
        def pair(k, _):
            hooks(k)
            i = BACK // 2 - 1 - k
            keys = jnp.concatenate([tile(2 * g, 2 * i), tile(2 * g, 2 * i + 1)], axis=0)

            def head(h, _):
                s = score(g, h, keys)
                best = peak[h]
                for c in range(4):
                    index = column + (i * 512 + c * D)
                    allowed = index[None] >= start_ref[...].reshape(T // 8, 8, D)
                    part = jnp.where(allowed.reshape(T, D), s[:, c * D : (c + 1) * D], NEG)
                    scores[i * 2 + c // 2, h, :, (c % 2) * D : (c % 2 + 1) * D] = part
                    best = jnp.maximum(best, part)
                peak[h] = best
                return 0

            lax.fori_loop(0, PER, head, 0, unroll=True)
            return 0

        keys = tile(2 * g, BACK)

        def diagonal(h, _):
            s = score(g, h, keys)
            row = lax.broadcasted_iota(jnp.int32, (T, D), 0)
            best = jnp.full((T, D), NEG, F32)
            for c in range(2):
                index = lax.broadcasted_iota(jnp.int32, (T, D), 1) + c * D
                allowed = (index + BACK * T >= start_ref[...]) & (index <= row)
                part = jnp.where(allowed, s[:, c * D : (c + 1) * D], NEG)
                scores[BACK, h, :, c * D : (c + 1) * D] = part
                best = jnp.maximum(best, part)
            peak[h] = best
            return 0

        lax.fori_loop(0, PER, diagonal, 0, unroll=True)
        lax.fori_loop(0, BACK // 2, pair, 0)

    def out_copy(head, d):
        to = (z + d) % N_KV
        return pltpu.make_async_remote_copy(
            src_ref=obuf.at[head, pl.ds(to * 64, 64), :],
            dst_ref=out_ref.at[:, pl.ds(pl.multiple_of((z * 16 + head) * D, D), D)],
            send_sem=osend.at[0],
            recv_sem=orecv.at[0],
            device_id={"kv": to},
            device_id_type=MESH,
        )

    def pass2(g, hooks):
        values = jnp.concatenate([tile(2 * g + 1, i) for i in range(BACK + 1)], axis=0)

        def head(h, _):
            hooks(h)
            top = jnp.max(peak[h], axis=1, keepdims=True)
            wide = jnp.broadcast_to(top, (T, D))
            total = jnp.zeros((T, D), F32)
            probs = []
            for i in range(BACK + 1):
                for c in range(2):
                    p = jnp.exp2((scores[i, h, :, c * D : (c + 1) * D] - wide) * C2)
                    total = total + p
                    probs.append(p.astype(BF))
            mixed = jnp.dot(
                jnp.concatenate(probs, axis=1), values, preferred_element_type=F32
            )
            row_sum = jnp.sum(total, axis=1, keepdims=True)
            here = g * PER + h
            obuf[here] = (mixed / row_sum).astype(BF)
            norm = top * SCALE + jnp.log(row_sum)
            lse_own[...] = jnp.where(lane == here, norm, lse_own[...])
            for d in range(1, N_KV):
                out_copy(here, d).start()
            out_ref[:, pl.ds(pl.multiple_of((z * 16 + here) * D, D), D)] = obuf[
                here, pl.ds(pl.multiple_of(z * 64, 64), 64), :
            ]
            return 0

        lax.fori_loop(0, PER, head, 0)

    lse_own[...] = jnp.zeros((T, D), F32)
    def hooks_of(table):
        def hooks(k):
            for step, calls in table.items():

                @pl.when(k == step)
                def _():
                    for call, *where in calls:
                        call(*where)

        return hooks

    pass1(0, hooks_of({
        0: [(stage_a, 2)],
        1: [(stage_t, 1, 2), (stage_t, 1, 1)],
        2: [(stage_t, 1, 0)],
        4: [(settle, 0, 0), (stage_b, 2)],
        6: [(stage_a, 3)],
    }))
    for row in range(3):
        settle(1, row)
    pass2(0, hooks_of({
        0: [(stage_t, 2, 2), (stage_t, 2, 1)],
        1: [(stage_t, 2, 0)],
        2: [(stage_b, 3)],
        5: [(stage_t, 3, 2), (stage_t, 3, 1)],
        6: [(stage_t, 3, 0)],
    }))
    for row in range(3):
        settle(2, row)
    pass1(1, lambda k: None)
    for row in range(3):
        settle(3, row)
    pass2(1, lambda h: None)

    spread_rows = (
        lax.broadcasted_iota(jnp.int32, (T, N_TOK), 0) // 8
        == lax.broadcasted_iota(jnp.int32, (T, N_TOK), 1)
    ).astype(F32)
    plans = lax.dot_general(
        spread_rows.astype(BF), plan_ref[...].astype(F32).astype(BF),
        (((1,), (1,)), ((), ())), preferred_element_type=F32,
    )
    mine = lax.broadcasted_iota(jnp.int32, (T, N_TOK), 1) == j
    block = jnp.sum(jnp.where(mine, plans, 0.0), axis=1, keepdims=True).astype(jnp.int32)
    wanted = block * 8 + lax.broadcasted_iota(jnp.int32, (T, T), 0) % 8
    pick = (wanted == lax.broadcasted_iota(jnp.int32, (T, T), 1)).astype(F32).astype(BF)
    rest = lse_own[...]
    ordered = jnp.zeros((T, D), F32)
    for _ in range(3):
        piece = rest.astype(BF)
        rest = rest - piece.astype(F32)
        ordered = ordered + jnp.dot(pick, piece, preferred_element_type=F32)
    lse_send[...] = ordered.reshape(N_TOK, 8, D)
    lse_recv[j] = lse_send[j]

    def lse_copy(d):
        to = (j + d) % N_TOK
        return pltpu.make_async_remote_copy(
            src_ref=lse_send.at[to],
            dst_ref=lse_recv.at[j],
            send_sem=lsend.at[0],
            recv_sem=lrecv.at[0],
            device_id={"tok": to},
            device_id_type=MESH,
        )

    def lse_start(d, _):
        lse_copy(d).start()
        return 0

    def finish(part, sem):
        pltpu.make_async_copy(part, part, sem.at[0]).wait()

    lax.fori_loop(1, N_TOK, lse_start, 0)
    for t in range(4):
        drain(t)
    finish(lse_recv.at[pl.ds(0, N_TOK - 1)], lrecv)
    lse_ref[...] = lse_recv[...].reshape(T, D).T[:16, :]
    finish(lse_send.at[pl.ds(0, N_TOK - 1)], lsend)
    finish(obuf.at[pl.ds(0, 12)], osend)
    finish(out_ref.at[:, pl.ds(0, 48 * D)], orecv)


def body(queries, key_states, value_states, doc_lengths, block_plan):
    half = np.power(THETA, -(np.arange(D // 2) * 2.0 / D)).astype(np.float32)
    freq = jnp.asarray(np.concatenate([half, half])[None, :])
    vmem = pl.BlockSpec(memory_space=pltpu.VMEM)
    far = pl.BlockSpec(memory_space=pl.ANY)
    return pl.pallas_call(
        kernel,
        out_shape=(
            jax.ShapeDtypeStruct((T // N_KV, N_KV * GROUPS * PER * D), BF),
            jax.ShapeDtypeStruct((GROUPS * PER, T), F32),
        ),
        in_specs=[pl.BlockSpec(memory_space=pltpu.SMEM)] + [vmem] * 2 + [far] * 3,
        out_specs=(vmem, vmem),
        scratch_shapes=[
            pltpu.VMEM((T, GROUPS * PER * D), BF),
            pltpu.VMEM((T, GROUPS * D), BF),
            pltpu.VMEM((T, GROUPS * D), BF),
            pltpu.VMEM((4, SLOTS, T, D), BF),
            pltpu.VMEM((GROUPS * PER, T, D), BF),
            pltpu.VMEM((BACK + 1, PER, T, T), F32),
            pltpu.VMEM((PER, T, D), F32),
            pltpu.VMEM((GROUPS * PER, T, D), BF),
            pltpu.VMEM((T, D), jnp.int32),
            pltpu.VMEM((T, D), F32),
            pltpu.VMEM((T, D), F32),
            pltpu.VMEM((T, D), F32),
            pltpu.VMEM((N_TOK, 8, D), F32),
            pltpu.VMEM((N_TOK, 8, D), F32),
            pltpu.SemaphoreType.DMA((3,)),
            pltpu.SemaphoreType.DMA((4,)),
            pltpu.SemaphoreType.DMA((4, SLOTS)),
            pltpu.SemaphoreType.DMA((4, 3)),
            pltpu.SemaphoreType.DMA((1,)),
            pltpu.SemaphoreType.DMA((1,)),
            pltpu.SemaphoreType.DMA((1,)),
            pltpu.SemaphoreType.DMA((1,)),
        ],
        compiler_params=pltpu.CompilerParams(
            collective_id=0, has_side_effects=True, vmem_limit_bytes=60 << 20
        ),
    )(doc_lengths, freq, block_plan, queries, key_states, value_states)


def solution(mesh):
    return jax.shard_map(
        body,
        mesh=mesh,
        in_specs=(P("tok", "kv"), P("tok", "kv"), P("tok", "kv"), P(), P()),
        out_specs=(P(("tok", "kv"), None), P("kv", "tok")),
        check_vma=False,
    )
```

```python
import functools
import math

import jax
import jax.numpy as jnp
import numpy as np
from jax import lax
from jax.experimental import pallas as pl
from jax.experimental.pallas import tpu as pltpu
from jax.sharding import PartitionSpec as P

D = 128
T = 256
GROUPS = 2
PER = 8
N_TOK = 32
N_KV = 4
DOCS = 16
BACK = 16
SLOTS = 24
NEG = -1e30
THETA = 500000.0
SCALE = 1.0 / math.sqrt(D)
C2 = SCALE * math.log2(math.e)
MESH = pl.DeviceIdType.MESH
BF = jnp.bfloat16
F32 = jnp.float32


def kernel(
    doc_ref, freq_ref, plan_ref, q_hbm, k_hbm, v_hbm,
    out_ref, lse_ref,
    q_ref, k_ref, v_ref, kv, qrot, scores, peak, obuf, start_ref, cos_ref, sin_ref, lse_own, lse_send, lse_recv,
    insem, ksend, krecv, trecv, osend, orecv, lsend, lrecv,
):
    j = lax.axis_index("tok")
    z = lax.axis_index("kv")
    core = j % 2
    x = (j // 2) % 4
    y = j // 8
    pos = j % 8
    own = core * 4 + x

    loads = [
        pltpu.make_async_copy(k_hbm, k_ref, insem.at[0]),
        pltpu.make_async_copy(v_hbm, v_ref, insem.at[1]),
        pltpu.make_async_copy(q_hbm, q_ref, insem.at[2]),
    ]
    for load in loads:
        load.start()

    def tok_of(y_, x_, core_):
        return ((y_ % 4) * 4 + (x_ % 4)) * 2 + core_

    barrier = pltpu.get_barrier_semaphore()

    def greet(d, _):
        pl.semaphore_signal(
            barrier, inc=1, device_id={"tok": (j + d) % N_TOK}, device_id_type=MESH
        )
        return 0

    lax.fori_loop(1, N_TOK, greet, 0)
    for d in range(1, N_KV):
        pl.semaphore_signal(
            barrier, inc=1, device_id={"kv": (z + d) % N_KV}, device_id_type=MESH
        )

    token = j * T + lax.broadcasted_iota(jnp.int32, (T, D), 0)
    lane = lax.broadcasted_iota(jnp.int32, (T, D), 1)
    start = jnp.zeros((T, D), jnp.int32)
    end = jnp.int32(0)
    for i in range(DOCS):
        end = end + doc_ref[i]
        start = jnp.where(token >= end, end, start)
    start_ref[...] = start - (j - BACK) * T
    angle = (token - start).astype(F32) * freq_ref[...]
    cos_ref[...] = jnp.cos(angle)
    sine = jnp.sin(angle)
    sin_ref[...] = jnp.where(lane < D // 2, -sine, sine)

    def rotate(block):
        wide = block.astype(F32)
        return (wide * cos_ref[...] + pltpu.roll(wide, D // 2, 1) * sin_ref[...]).astype(BF)

    loads[0].wait()
    loads[1].wait()
    for g in range(GROUPS):
        kv[2 * g, 16 + own] = rotate(k_ref[:, g * D : (g + 1) * D])
        kv[2 * g + 1, 16 + own] = v_ref[:, g * D : (g + 1) * D]

    pl.semaphore_wait(barrier, N_TOK - 1 + N_KV - 1)

    def copy(t, source, target, to):
        return pltpu.make_async_remote_copy(
            src_ref=kv.at[t, source],
            dst_ref=kv.at[t, target],
            send_sem=ksend.at[t],
            recv_sem=krecv.at[t, target],
            device_id={"tok": to},
            device_id_type=MESH,
        )

    def share(t, row):
        mine = pl.ds(row * 8 + core * 4, 4)
        return pltpu.make_async_remote_copy(
            src_ref=kv.at[t, mine],
            dst_ref=kv.at[t, mine],
            send_sem=ksend.at[t],
            recv_sem=trecv.at[t, row],
            device_id={"tok": tok_of(y, x, 1 - core)},
            device_id_type=MESH,
        )

    def needs(row, source_x, target_x):
        return (target_x > source_x) if row == 2 else (target_x < source_x)

    def spread(t, row):
        slot = row * 8 + own
        for d in (1, 3, 2):
            target_x = (x + d) % 4

            def send():
                copy(t, slot, slot, tok_of(y, target_x, core)).start()

            if row == 1:
                send()
            else:
                pl.when(needs(row, x, target_x))(send)

    def stage_a(t):
        for d in (1, 2):
            copy(t, 16 + own, 16 - 8 * d + own, tok_of(y + d, x, core)).start()
        spread(t, 2)

    def stage_b(t):
        for row in (1, 0):
            copy(t, 0, row * 8 + own, j).wait_recv()
            spread(t, row)

    def stage_t(t, row):
        for d in (1, 3, 2):
            source_x = (x + 4 - d) % 4

            def arrive():
                copy(t, 0, row * 8 + core * 4 + source_x, j).wait_recv()

            if row == 1:
                arrive()
            else:
                pl.when(needs(row, source_x, x))(arrive)
        share(t, row).start()

    def settle(t, row):
        pltpu.make_async_copy(
            kv.at[t, pl.ds(0, 4)], kv.at[t, pl.ds(row * 8, 4)], trecv.at[t, row]
        ).wait()

    def drain(t):
        part = kv.at[t, pl.ds(0, 20)]
        pltpu.make_async_copy(part, part, ksend.at[t]).wait()

    def turn(h, _):
        lanes = pl.ds(pl.multiple_of(h * D, D), D)
        qrot[h] = rotate(q_ref[:, lanes])
        return 0

    stage_a(0)
    loads[2].wait()
    lax.fori_loop(0, PER, turn, 0)
    stage_b(0)
    stage_a(1)
    lax.fori_loop(PER, 2 * PER, turn, 0)
    stage_t(0, 2)
    stage_t(0, 1)
    stage_b(1)
    stage_t(0, 0)
    settle(0, 2)
    settle(0, 1)

    def tile(t, i):
        at = pos + i
        place = at % 8
        return kv[t, (at // 8) * 8 + (place % 2) * 4 + place // 2]

    column = lax.broadcasted_iota(jnp.int32, (8, D), 1)

    def score(g, h, keys):
        return lax.dot_general(
            qrot[g * PER + h], keys, (((1,), (1,)), ((), ())), preferred_element_type=F32
        )

    def pass1(g, lo, hi):
        def pair(k, _):
            i = BACK // 4 - 1 - k
            keys = jnp.concatenate([tile(2 * g, 4 * i + e) for e in range(4)], axis=0)

            def head(h, _):
                s = score(g, h, keys)
                best = peak[h]
                for c in range(8):
                    index = column + (i * 1024 + c * D)
                    allowed = index[None] >= start_ref[...].reshape(T // 8, 8, D)
                    part = jnp.where(allowed.reshape(T, D), s[:, c * D : (c + 1) * D], NEG)
                    scores[i * 4 + c // 2, h, :, (c % 2) * D : (c % 2 + 1) * D] = part
                    best = jnp.maximum(best, part)
                peak[h] = best
                return 0

            lax.fori_loop(0, PER, head, 0, unroll=True)
            return 0

        keys = tile(2 * g, BACK)

        def diagonal(h, _):
            s = score(g, h, keys)
            row = lax.broadcasted_iota(jnp.int32, (T, D), 0)
            best = jnp.full((T, D), NEG, F32)
            for c in range(2):
                index = lax.broadcasted_iota(jnp.int32, (T, D), 1) + c * D
                allowed = (index + BACK * T >= start_ref[...]) & (index <= row)
                part = jnp.where(allowed, s[:, c * D : (c + 1) * D], NEG)
                scores[BACK, h, :, c * D : (c + 1) * D] = part
                best = jnp.maximum(best, part)
            peak[h] = best
            return 0

        if lo == 0:
            lax.fori_loop(0, PER, diagonal, 0, unroll=True)
        lax.fori_loop(lo, hi, pair, 0)

    def out_lanes(two):
        return pl.ds(pl.multiple_of((z * 8 + two) * 2 * D, 2 * D), 2 * D)

    def out_copy(two, d):
        to = (z + d) % N_KV
        return pltpu.make_async_remote_copy(
            src_ref=obuf.at[two, pl.ds(to * 64, 64), :],
            dst_ref=out_ref.at[:, out_lanes(two)],
            send_sem=osend.at[0],
            recv_sem=orecv.at[0],
            device_id={"kv": to},
            device_id_type=MESH,
        )

    def pass2(g, lo, hi):
        values = jnp.concatenate([tile(2 * g + 1, i) for i in range(BACK + 1)], axis=0)

        def pair(k, _):
            probs, tops, sums = [], [], []
            for e in range(2):
                h = 2 * k + e
                top = jnp.max(peak[h], axis=1, keepdims=True)
                wide = jnp.broadcast_to(top, (T, D))
                total = jnp.zeros((T, D), F32)
                parts = []
                for i in range(BACK + 1):
                    for c in range(2):
                        p = jnp.exp2((scores[i, h, :, c * D : (c + 1) * D] - wide) * C2)
                        total = total + p
                        parts.append(p.astype(BF))
                probs.append(jnp.concatenate(parts, axis=1))
                tops.append(top)
                sums.append(jnp.sum(total, axis=1, keepdims=True))
            mixed = jnp.dot(
                jnp.concatenate(probs, axis=0), values, preferred_element_type=F32
            )
            here = g * (PER // 2) + k
            norms = lse_own[...]
            for e in range(2):
                part = mixed[e * T : (e + 1) * T] / sums[e]
                obuf[here, :, e * D : (e + 1) * D] = part.astype(BF)
                norms = jnp.where(lane == 2 * here + e, tops[e] * SCALE + jnp.log(sums[e]), norms)
            lse_own[...] = norms
            for d in range(1, N_KV):
                out_copy(here, d).start()
            out_ref[:, out_lanes(here)] = obuf[here, pl.ds(pl.multiple_of(z * 64, 64), 64), :]
            return 0

        lax.fori_loop(lo, hi, pair, 0)

    lse_own[...] = jnp.zeros((T, D), F32)
    stage_a(2)
    stage_a(3)
    pass1(0, 0, 2)
    stage_t(1, 2)
    stage_t(1, 1)
    settle(0, 0)
    pass1(0, 2, 4)
    stage_t(1, 0)
    stage_b(2)
    stage_b(3)
    for row in range(3):
        settle(1, row)
    pass2(0, 0, 4)
    for row in (2, 1, 0):
        stage_t(2, row)
    for row in (2, 1, 0):
        stage_t(3, row)
    for row in range(3):
        settle(2, row)
    pass1(1, 0, 4)
    for row in range(3):
        settle(3, row)
    pass2(1, 0, 4)

    spread_rows = (
        lax.broadcasted_iota(jnp.int32, (T, N_TOK), 0) // 8
        == lax.broadcasted_iota(jnp.int32, (T, N_TOK), 1)
    ).astype(F32)
    plans = lax.dot_general(
        spread_rows.astype(BF), plan_ref[...].astype(F32).astype(BF),
        (((1,), (1,)), ((), ())), preferred_element_type=F32,
    )
    mine = lax.broadcasted_iota(jnp.int32, (T, N_TOK), 1) == j
    block = jnp.sum(jnp.where(mine, plans, 0.0), axis=1, keepdims=True).astype(jnp.int32)
    wanted = block * 8 + lax.broadcasted_iota(jnp.int32, (T, T), 0) % 8
    pick = (wanted == lax.broadcasted_iota(jnp.int32, (T, T), 1)).astype(F32).astype(BF)
    rest = lse_own[...]
    ordered = jnp.zeros((T, D), F32)
    for _ in range(3):
        piece = rest.astype(BF)
        rest = rest - piece.astype(F32)
        ordered = ordered + jnp.dot(pick, piece, preferred_element_type=F32)
    lse_send[...] = ordered.reshape(N_TOK, 8, D)
    lse_recv[j] = lse_send[j]

    def lse_copy(d):
        to = (j + d) % N_TOK
        return pltpu.make_async_remote_copy(
            src_ref=lse_send.at[to],
            dst_ref=lse_recv.at[j],
            send_sem=lsend.at[0],
            recv_sem=lrecv.at[0],
            device_id={"tok": to},
            device_id_type=MESH,
        )

    def lse_start(d, _):
        lse_copy(d).start()
        return 0

    def finish(part, sem):
        pltpu.make_async_copy(part, part, sem.at[0]).wait()

    lax.fori_loop(1, N_TOK, lse_start, 0)
    for t in range(4):
        drain(t)
    finish(lse_recv.at[pl.ds(0, N_TOK - 1)], lrecv)
    lse_ref[...] = lse_recv[...].reshape(T, D).T[:16, :]
    finish(lse_send.at[pl.ds(0, N_TOK - 1)], lsend)
    finish(obuf.at[pl.ds(0, 6)], osend)
    finish(out_ref.at[:, pl.ds(0, 48 * D)], orecv)


def body(queries, key_states, value_states, doc_lengths, block_plan):
    half = np.power(THETA, -(np.arange(D // 2) * 2.0 / D)).astype(np.float32)
    freq = jnp.asarray(np.concatenate([half, half])[None, :])
    vmem = pl.BlockSpec(memory_space=pltpu.VMEM)
    far = pl.BlockSpec(memory_space=pl.ANY)
    return pl.pallas_call(
        kernel,
        out_shape=(
            pltpu.VMEM((T // N_KV, N_KV * GROUPS * PER * D), BF),
            pltpu.VMEM((GROUPS * PER, T), F32),
        ),
        in_specs=[pl.BlockSpec(memory_space=pltpu.SMEM)] + [vmem] * 2 + [far] * 3,
        out_specs=(vmem, vmem),
        scratch_shapes=[
            pltpu.VMEM((T, GROUPS * PER * D), BF),
            pltpu.VMEM((T, GROUPS * D), BF),
            pltpu.VMEM((T, GROUPS * D), BF),
            pltpu.VMEM((4, SLOTS, T, D), BF),
            pltpu.VMEM((GROUPS * PER, T, D), BF),
            pltpu.VMEM((BACK + 1, PER, T, T), F32),
            pltpu.VMEM((PER, T, D), F32),
            pltpu.VMEM((GROUPS * PER // 2, T, 2 * D), BF),
            pltpu.VMEM((T, D), jnp.int32),
            pltpu.VMEM((T, D), F32),
            pltpu.VMEM((T, D), F32),
            pltpu.VMEM((T, D), F32),
            pltpu.VMEM((N_TOK, 8, D), F32),
            pltpu.VMEM((N_TOK, 8, D), F32),
            pltpu.SemaphoreType.DMA((3,)),
            pltpu.SemaphoreType.DMA((4,)),
            pltpu.SemaphoreType.DMA((4, SLOTS)),
            pltpu.SemaphoreType.DMA((4, 3)),
            pltpu.SemaphoreType.DMA((1,)),
            pltpu.SemaphoreType.DMA((1,)),
            pltpu.SemaphoreType.DMA((1,)),
            pltpu.SemaphoreType.DMA((1,)),
        ],
        compiler_params=pltpu.CompilerParams(
            collective_id=0, has_side_effects=True, vmem_limit_bytes=58 << 20
        ),
    )(doc_lengths, freq, block_plan, queries, key_states, value_states)


def solution(mesh):
    return jax.shard_map(
        body,
        mesh=mesh,
        in_specs=(P("tok", "kv"), P("tok", "kv"), P("tok", "kv"), P(), P()),
        out_specs=(P(("tok", "kv"), None), P("kv", "tok")),
        check_vma=False,
    )
```

```python
import functools
import math

import jax
import jax.numpy as jnp
import numpy as np
from jax import lax
from jax.experimental import pallas as pl
from jax.experimental.pallas import tpu as pltpu
from jax.sharding import PartitionSpec as P

D = 128
T = 256
GROUPS = 2
PER = 8
N_TOK = 32
N_KV = 4
DOCS = 16
BACK = 16
SLOTS = 24
NEG = -1e30
THETA = 500000.0
SCALE = 1.0 / math.sqrt(D)
C2 = SCALE * math.log2(math.e)
MESH = pl.DeviceIdType.MESH
BF = jnp.bfloat16
F32 = jnp.float32


def kernel(
    doc_ref, freq_ref, plan_ref, q_hbm, k_hbm, v_hbm,
    out_ref, lse_ref,
    q_ref, k_ref, v_ref, kv, qrot, scores, peak, obuf, start_ref, cos_ref, sin_ref, lse_own, lse_send, lse_recv,
    insem, ksend, krecv, trecv, osend, orecv, lsend, lrecv,
):
    j = lax.axis_index("tok")
    z = lax.axis_index("kv")
    core = j % 2
    x = (j // 2) % 4
    y = j // 8
    pos = j % 8
    own = core * 4 + x

    loads = [
        pltpu.make_async_copy(k_hbm, k_ref, insem.at[0]),
        pltpu.make_async_copy(v_hbm, v_ref, insem.at[1]),
        pltpu.make_async_copy(q_hbm, q_ref, insem.at[2]),
    ]
    for load in loads:
        load.start()

    def tok_of(y_, x_, core_):
        return ((y_ % 4) * 4 + (x_ % 4)) * 2 + core_

    barrier = pltpu.get_barrier_semaphore()

    def greet(d, _):
        pl.semaphore_signal(
            barrier, inc=1, device_id={"tok": (j + d) % N_TOK}, device_id_type=MESH
        )
        return 0

    lax.fori_loop(1, N_TOK, greet, 0)
    for d in range(1, N_KV):
        pl.semaphore_signal(
            barrier, inc=1, device_id={"kv": (z + d) % N_KV}, device_id_type=MESH
        )

    token = j * T + lax.broadcasted_iota(jnp.int32, (T, D), 0)
    lane = lax.broadcasted_iota(jnp.int32, (T, D), 1)
    start = jnp.zeros((T, D), jnp.int32)
    end = jnp.int32(0)
    for i in range(DOCS):
        end = end + doc_ref[i]
        start = jnp.where(token >= end, end, start)
    start_ref[...] = start - (j - BACK) * T
    angle = (token - start).astype(F32) * freq_ref[...]
    cos_ref[...] = jnp.cos(angle)
    sine = jnp.sin(angle)
    sin_ref[...] = jnp.where(lane < D // 2, -sine, sine)

    def rotate(block):
        wide = block.astype(F32)
        return (wide * cos_ref[...] + pltpu.roll(wide, D // 2, 1) * sin_ref[...]).astype(BF)

    loads[0].wait()
    loads[1].wait()
    for g in range(GROUPS):
        kv[2 * g, 16 + own] = rotate(k_ref[:, g * D : (g + 1) * D])
        kv[2 * g + 1, 16 + own] = v_ref[:, g * D : (g + 1) * D]

    pl.semaphore_wait(barrier, N_TOK - 1 + N_KV - 1)

    def copy(t, source, target, to):
        return pltpu.make_async_remote_copy(
            src_ref=kv.at[t, source],
            dst_ref=kv.at[t, target],
            send_sem=ksend.at[t],
            recv_sem=krecv.at[t, target],
            device_id={"tok": to},
            device_id_type=MESH,
        )

    def share(t, row):
        mine = pl.ds(row * 8 + core * 4, 4)
        return pltpu.make_async_remote_copy(
            src_ref=kv.at[t, mine],
            dst_ref=kv.at[t, mine],
            send_sem=ksend.at[t],
            recv_sem=trecv.at[t, row],
            device_id={"tok": tok_of(y, x, 1 - core)},
            device_id_type=MESH,
        )

    def needs(row, source_x, target_x):
        return (target_x > source_x) if row == 2 else (target_x < source_x)

    def spread(t, row):
        slot = row * 8 + own
        for d in (1, 3, 2):
            target_x = (x + d) % 4

            def send():
                copy(t, slot, slot, tok_of(y, target_x, core)).start()

            if row == 1:
                send()
            else:
                pl.when(needs(row, x, target_x))(send)

    def stage_a(t):
        for d in (1, 2):
            copy(t, 16 + own, 16 - 8 * d + own, tok_of(y + d, x, core)).start()
        spread(t, 2)

    def stage_b(t):
        for row in (1, 0):
            copy(t, 0, row * 8 + own, j).wait_recv()
            spread(t, row)

    def stage_t(t, row):
        for d in (1, 3, 2):
            source_x = (x + 4 - d) % 4

            def arrive():
                copy(t, 0, row * 8 + core * 4 + source_x, j).wait_recv()

            if row == 1:
                arrive()
            else:
                pl.when(needs(row, source_x, x))(arrive)
        share(t, row).start()

    def settle(t, row):
        pltpu.make_async_copy(
            kv.at[t, pl.ds(0, 4)], kv.at[t, pl.ds(row * 8, 4)], trecv.at[t, row]
        ).wait()

    def drain(t):
        part = kv.at[t, pl.ds(0, 20)]
        pltpu.make_async_copy(part, part, ksend.at[t]).wait()

    def turn(h, _):
        lanes = pl.ds(pl.multiple_of(h * D, D), D)
        qrot[h] = rotate(q_ref[:, lanes])
        return 0

    def tile(t, i):
        at = pos + i
        place = at % 8
        return kv[t, (at // 8) * 8 + (place % 2) * 4 + place // 2]

    column = lax.broadcasted_iota(jnp.int32, (8, D), 1)

    def score(g, h, keys):
        return lax.dot_general(
            qrot[g * PER + h], keys, (((1,), (1,)), ((), ())), preferred_element_type=F32
        )

    def pass1(g, lo, hi):
        def pair(k, _):
            i = BACK // 4 - 1 - k
            keys = jnp.concatenate([tile(2 * g, 4 * i + e) for e in range(4)], axis=0)

            def head(h, _):
                s = score(g, h, keys)
                best = peak[h]
                for c in range(8):
                    index = column + (i * 1024 + c * D)
                    allowed = index[None] >= start_ref[...].reshape(T // 8, 8, D)
                    part = jnp.where(allowed.reshape(T, D), s[:, c * D : (c + 1) * D], NEG)
                    scores[i * 4 + c // 2, h, :, (c % 2) * D : (c % 2 + 1) * D] = part
                    best = jnp.maximum(best, part)
                peak[h] = best
                return 0

            lax.fori_loop(0, PER, head, 0, unroll=True)
            return 0

        lax.fori_loop(lo, hi, pair, 0)

    def pass1_own(g):
        keys = tile(2 * g, BACK)

        def diagonal(h, _):
            s = score(g, h, keys)
            row = lax.broadcasted_iota(jnp.int32, (T, D), 0)
            best = jnp.full((T, D), NEG, F32)
            for c in range(2):
                index = lax.broadcasted_iota(jnp.int32, (T, D), 1) + c * D
                allowed = (index + BACK * T >= start_ref[...]) & (index <= row)
                part = jnp.where(allowed, s[:, c * D : (c + 1) * D], NEG)
                scores[BACK, h, :, c * D : (c + 1) * D] = part
                best = jnp.maximum(best, part)
            peak[h] = best
            return 0

        lax.fori_loop(0, PER, diagonal, 0, unroll=True)

    def out_lanes(two):
        return pl.ds(pl.multiple_of((z * 8 + two) * 2 * D, 2 * D), 2 * D)

    def out_copy(two, d):
        to = (z + d) % N_KV
        return pltpu.make_async_remote_copy(
            src_ref=obuf.at[two, pl.ds(to * 64, 64), :],
            dst_ref=out_ref.at[:, out_lanes(two)],
            send_sem=osend.at[0],
            recv_sem=orecv.at[0],
            device_id={"kv": to},
            device_id_type=MESH,
        )

    def pass2(g, lo, hi):
        values = jnp.concatenate([tile(2 * g + 1, i) for i in range(BACK + 1)], axis=0)
        values = jnp.concatenate([values, jnp.ones_like(values)], axis=1)

        def pair(k, _):
            probs, tops = [], []
            for e in range(2):
                h = 2 * k + e
                top = jnp.max(peak[h], axis=1, keepdims=True)
                wide = jnp.broadcast_to(top, (T, D))
                parts = []
                for i in range(BACK + 1):
                    for c in range(2):
                        p = jnp.exp2((scores[i, h, :, c * D : (c + 1) * D] - wide) * C2)
                        parts.append(p.astype(BF))
                probs.append(jnp.concatenate(parts, axis=1))
                tops.append(top)
            mixed = jnp.dot(
                jnp.concatenate(probs, axis=0), values, preferred_element_type=F32
            )
            here = g * (PER // 2) + k
            norms = lse_own[...]
            for e in range(2):
                row_sum = mixed[e * T : (e + 1) * T, D:]
                part = mixed[e * T : (e + 1) * T, :D] / row_sum
                obuf[here, :, e * D : (e + 1) * D] = part.astype(BF)
                norms = jnp.where(lane == 2 * here + e, tops[e] * SCALE + jnp.log(row_sum), norms)
            lse_own[...] = norms
            for d in range(1, N_KV):
                out_copy(here, d).start()
            out_ref[:, out_lanes(here)] = obuf[here, pl.ds(pl.multiple_of(z * 64, 64), 64), :]
            return 0

        lax.fori_loop(lo, hi, pair, 0)

    lse_own[...] = jnp.zeros((T, D), F32)
    stage_a(0)
    loads[2].wait()
    lax.fori_loop(0, PER, turn, 0)
    stage_b(0)
    stage_a(1)
    pass1_own(0)
    lax.fori_loop(PER, 2 * PER, turn, 0)
    stage_t(0, 2)
    stage_t(0, 1)
    stage_b(1)
    stage_t(0, 0)
    settle(0, 2)
    settle(0, 1)
    stage_a(2)
    stage_a(3)
    pass1(0, 0, 2)
    stage_t(1, 2)
    stage_t(1, 1)
    settle(0, 0)
    pass1(0, 2, 3)
    stage_t(1, 0)
    stage_b(2)
    pass1(0, 3, 4)
    for row in range(3):
        settle(1, row)
    stage_b(3)
    pass2(0, 0, 3)
    for row in (2, 1, 0):
        stage_t(2, row)
    pass2(0, 3, 4)
    for row in range(3):
        settle(2, row)
    pass1_own(1)
    pass1(1, 0, 2)
    for row in (2, 1, 0):
        stage_t(3, row)
    pass1(1, 2, 4)
    for row in range(3):
        settle(3, row)
    pass2(1, 0, 4)

    spread_rows = (
        lax.broadcasted_iota(jnp.int32, (T, N_TOK), 0) // 8
        == lax.broadcasted_iota(jnp.int32, (T, N_TOK), 1)
    ).astype(F32)
    plans = lax.dot_general(
        spread_rows.astype(BF), plan_ref[...].astype(F32).astype(BF),
        (((1,), (1,)), ((), ())), preferred_element_type=F32,
    )
    mine = lax.broadcasted_iota(jnp.int32, (T, N_TOK), 1) == j
    block = jnp.sum(jnp.where(mine, plans, 0.0), axis=1, keepdims=True).astype(jnp.int32)
    wanted = block * 8 + lax.broadcasted_iota(jnp.int32, (T, T), 0) % 8
    pick = (wanted == lax.broadcasted_iota(jnp.int32, (T, T), 1)).astype(F32).astype(BF)
    rest = lse_own[...]
    ordered = jnp.zeros((T, D), F32)
    for _ in range(3):
        piece = rest.astype(BF)
        rest = rest - piece.astype(F32)
        ordered = ordered + jnp.dot(pick, piece, preferred_element_type=F32)
    lse_send[...] = ordered.reshape(N_TOK, 8, D)
    lse_recv[j] = lse_send[j]

    def lse_copy(d):
        to = (j + d) % N_TOK
        return pltpu.make_async_remote_copy(
            src_ref=lse_send.at[to],
            dst_ref=lse_recv.at[j],
            send_sem=lsend.at[0],
            recv_sem=lrecv.at[0],
            device_id={"tok": to},
            device_id_type=MESH,
        )

    def lse_start(d, _):
        lse_copy(d).start()
        return 0

    def finish(part, sem):
        pltpu.make_async_copy(part, part, sem.at[0]).wait()

    lax.fori_loop(1, N_TOK, lse_start, 0)
    for t in range(4):
        drain(t)
    finish(lse_recv.at[pl.ds(0, N_TOK - 1)], lrecv)
    lse_ref[...] = lse_recv[...].reshape(T, D).T[:16, :]
    finish(lse_send.at[pl.ds(0, N_TOK - 1)], lsend)
    finish(obuf.at[pl.ds(0, 6)], osend)
    finish(out_ref.at[:, pl.ds(0, 48 * D)], orecv)


def body(queries, key_states, value_states, doc_lengths, block_plan):
    half = np.power(THETA, -(np.arange(D // 2) * 2.0 / D)).astype(np.float32)
    freq = jnp.asarray(np.concatenate([half, half])[None, :])
    vmem = pl.BlockSpec(memory_space=pltpu.VMEM)
    far = pl.BlockSpec(memory_space=pl.ANY)
    return pl.pallas_call(
        kernel,
        out_shape=(
            pltpu.VMEM((T // N_KV, N_KV * GROUPS * PER * D), BF),
            pltpu.VMEM((GROUPS * PER, T), F32),
        ),
        in_specs=[pl.BlockSpec(memory_space=pltpu.SMEM)] + [vmem] * 2 + [far] * 3,
        out_specs=(vmem, vmem),
        scratch_shapes=[
            pltpu.VMEM((T, GROUPS * PER * D), BF),
            pltpu.VMEM((T, GROUPS * D), BF),
            pltpu.VMEM((T, GROUPS * D), BF),
            pltpu.VMEM((4, SLOTS, T, D), BF),
            pltpu.VMEM((GROUPS * PER, T, D), BF),
            pltpu.VMEM((BACK + 1, PER, T, T), F32),
            pltpu.VMEM((PER, T, D), F32),
            pltpu.VMEM((GROUPS * PER // 2, T, 2 * D), BF),
            pltpu.VMEM((T, D), jnp.int32),
            pltpu.VMEM((T, D), F32),
            pltpu.VMEM((T, D), F32),
            pltpu.VMEM((T, D), F32),
            pltpu.VMEM((N_TOK, 8, D), F32),
            pltpu.VMEM((N_TOK, 8, D), F32),
            pltpu.SemaphoreType.DMA((3,)),
            pltpu.SemaphoreType.DMA((4,)),
            pltpu.SemaphoreType.DMA((4, SLOTS)),
            pltpu.SemaphoreType.DMA((4, 3)),
            pltpu.SemaphoreType.DMA((1,)),
            pltpu.SemaphoreType.DMA((1,)),
            pltpu.SemaphoreType.DMA((1,)),
            pltpu.SemaphoreType.DMA((1,)),
        ],
        compiler_params=pltpu.CompilerParams(
            collective_id=0, has_side_effects=True, vmem_limit_bytes=58 << 20
        ),
    )(doc_lengths, freq, block_plan, queries, key_states, value_states)


def solution(mesh):
    return jax.shard_map(
        body,
        mesh=mesh,
        in_specs=(P("tok", "kv"), P("tok", "kv"), P("tok", "kv"), P(), P()),
        out_specs=(P(("tok", "kv"), None), P("kv", "tok")),
        check_vma=False,
    )
```

```python
import functools
import math

import jax
import jax.numpy as jnp
import numpy as np
from jax import lax
from jax.experimental import pallas as pl
from jax.experimental.pallas import tpu as pltpu
from jax.sharding import PartitionSpec as P

D = 128
T = 256
GROUPS = 2
PER = 8
N_TOK = 32
N_KV = 4
DOCS = 16
BACK = 16
SLOTS = 24
NEG = -1e30
THETA = 500000.0
SCALE = 1.0 / math.sqrt(D)
C2 = SCALE * math.log2(math.e)
MESH = pl.DeviceIdType.MESH
BF = jnp.bfloat16
F32 = jnp.float32


def kernel(
    doc_ref, freq_ref, plan_ref, q_hbm, k_hbm, v_hbm,
    out_ref, lse_ref,
    q_ref, k_ref, v_ref, kv, qrot, scores, peak, obuf, start_ref, cos_ref, sin_ref, lse_own, lse_send, lse_recv,
    insem, ksend, krecv, trecv, osend, orecv, lsend, lrecv,
):
    j = lax.axis_index("tok")
    z = lax.axis_index("kv")
    core = j % 2
    x = (j // 2) % 4
    y = j // 8
    pos = j % 8
    own = core * 4 + x

    loads = [
        pltpu.make_async_copy(k_hbm, k_ref, insem.at[0]),
        pltpu.make_async_copy(v_hbm, v_ref, insem.at[1]),
        pltpu.make_async_copy(q_hbm, q_ref, insem.at[2]),
    ]
    for load in loads:
        load.start()

    def tok_of(y_, x_, core_):
        return ((y_ % 4) * 4 + (x_ % 4)) * 2 + core_

    barrier = pltpu.get_barrier_semaphore()

    def greet(d, _):
        pl.semaphore_signal(
            barrier, inc=1, device_id={"tok": (j + d) % N_TOK}, device_id_type=MESH
        )
        return 0

    lax.fori_loop(1, N_TOK, greet, 0)
    for d in range(1, N_KV):
        pl.semaphore_signal(
            barrier, inc=1, device_id={"kv": (z + d) % N_KV}, device_id_type=MESH
        )

    token = j * T + lax.broadcasted_iota(jnp.int32, (T, D), 0)
    lane = lax.broadcasted_iota(jnp.int32, (T, D), 1)
    start = jnp.zeros((T, D), jnp.int32)
    end = jnp.int32(0)
    for i in range(DOCS):
        end = end + doc_ref[i]
        start = jnp.where(token >= end, end, start)
    start_ref[...] = start - (j - BACK) * T
    angle = (token - start).astype(F32) * freq_ref[...]
    cos_ref[...] = jnp.cos(angle)
    sine = jnp.sin(angle)
    sin_ref[...] = jnp.where(lane < D // 2, -sine, sine)

    def rotate(block):
        wide = block.astype(F32)
        return (wide * cos_ref[...] + pltpu.roll(wide, D // 2, 1) * sin_ref[...]).astype(BF)

    loads[0].wait()
    loads[1].wait()
    for g in range(GROUPS):
        kv[2 * g, 16 + own] = rotate(k_ref[:, g * D : (g + 1) * D])
        kv[2 * g + 1, 16 + own] = v_ref[:, g * D : (g + 1) * D]

    pl.semaphore_wait(barrier, N_TOK - 1 + N_KV - 1)

    def copy(t, source, target, to):
        return pltpu.make_async_remote_copy(
            src_ref=kv.at[t, source],
            dst_ref=kv.at[t, target],
            send_sem=ksend.at[t],
            recv_sem=krecv.at[t, target],
            device_id={"tok": to},
            device_id_type=MESH,
        )

    def share(t, row):
        mine = pl.ds(row * 8 + core * 4, 4)
        return pltpu.make_async_remote_copy(
            src_ref=kv.at[t, mine],
            dst_ref=kv.at[t, mine],
            send_sem=ksend.at[t],
            recv_sem=trecv.at[t, row],
            device_id={"tok": tok_of(y, x, 1 - core)},
            device_id_type=MESH,
        )

    def needs(row, source_x, target_x):
        return (target_x > source_x) if row == 2 else (target_x < source_x)

    def spread(t, row):
        slot = row * 8 + own
        for d in (1, 3, 2):
            target_x = (x + d) % 4

            def send():
                copy(t, slot, slot, tok_of(y, target_x, core)).start()

            if row == 1:
                send()
            else:
                pl.when(needs(row, x, target_x))(send)

    def stage_a(t):
        for d in (1, 2):
            copy(t, 16 + own, 16 - 8 * d + own, tok_of(y + d, x, core)).start()
        spread(t, 2)

    def stage_b(t):
        for row in (1, 0):
            copy(t, 0, row * 8 + own, j).wait_recv()
            spread(t, row)

    def stage_t(t, row):
        for d in (1, 3, 2):
            source_x = (x + 4 - d) % 4

            def arrive():
                copy(t, 0, row * 8 + core * 4 + source_x, j).wait_recv()

            if row == 1:
                arrive()
            else:
                pl.when(needs(row, source_x, x))(arrive)
        share(t, row).start()

    def settle(t, row):
        pltpu.make_async_copy(
            kv.at[t, pl.ds(0, 4)], kv.at[t, pl.ds(row * 8, 4)], trecv.at[t, row]
        ).wait()

    def drain(t):
        part = kv.at[t, pl.ds(0, 20)]
        pltpu.make_async_copy(part, part, ksend.at[t]).wait()

    def turn(h, _):
        lanes = pl.ds(pl.multiple_of(h * D, D), D)
        qrot[h] = rotate(q_ref[:, lanes])
        return 0

    def tile(t, i):
        at = pos + i
        place = at % 8
        return kv[t, (at // 8) * 8 + (place % 2) * 4 + place // 2]

    column = lax.broadcasted_iota(jnp.int32, (8, D), 1)

    def score(g, h, keys):
        return lax.dot_general(
            qrot[g * PER + h], keys, (((1,), (1,)), ((), ())), preferred_element_type=F32
        )

    def pass1(g, lo, hi):
        def pair(k, _):
            i = BACK // 4 - 1 - k
            keys = jnp.concatenate([tile(2 * g, 4 * i + e) for e in range(4)], axis=0)

            def head(h, _):
                s = score(g, h, keys)
                best = peak[h]
                for c in range(8):
                    index = column + (i * 1024 + c * D)
                    allowed = index[None] >= start_ref[...].reshape(T // 8, 8, D)
                    part = jnp.where(allowed.reshape(T, D), s[:, c * D : (c + 1) * D], NEG)
                    scores[i * 4 + c // 2, h, :, (c % 2) * D : (c % 2 + 1) * D] = part
                    best = jnp.maximum(best, part)
                peak[h] = best
                return 0

            lax.fori_loop(0, PER, head, 0, unroll=True)
            return 0

        lax.fori_loop(lo, hi, pair, 0)

    def pass1_own(g):
        keys = tile(2 * g, BACK)

        def diagonal(h, _):
            s = score(g, h, keys)
            row = lax.broadcasted_iota(jnp.int32, (T, D), 0)
            best = jnp.full((T, D), NEG, F32)
            for c in range(2):
                index = lax.broadcasted_iota(jnp.int32, (T, D), 1) + c * D
                allowed = (index + BACK * T >= start_ref[...]) & (index <= row)
                part = jnp.where(allowed, s[:, c * D : (c + 1) * D], NEG)
                scores[BACK, h, :, c * D : (c + 1) * D] = part
                best = jnp.maximum(best, part)
            peak[h] = best
            return 0

        lax.fori_loop(0, PER, diagonal, 0, unroll=True)

    def out_lanes(two):
        return pl.ds(pl.multiple_of((z * 8 + two) * 2 * D, 2 * D), 2 * D)

    def out_copy(two, d):
        to = (z + d) % N_KV
        return pltpu.make_async_remote_copy(
            src_ref=obuf.at[two, pl.ds(to * 64, 64), :],
            dst_ref=out_ref.at[:, out_lanes(two)],
            send_sem=osend.at[0],
            recv_sem=orecv.at[0],
            device_id={"kv": to},
            device_id_type=MESH,
        )

    def pass2(g, lo, hi):
        values = jnp.concatenate([tile(2 * g + 1, i) for i in range(BACK + 1)], axis=0)
        values = jnp.concatenate([values, jnp.ones_like(values)], axis=1)

        def pair(k, _):
            probs, tops = [], []
            for e in range(2):
                h = 2 * k + e
                top = jnp.max(peak[h], axis=1, keepdims=True)
                wide = jnp.broadcast_to(top, (T, D))
                parts = []
                for i in range(BACK + 1):
                    for c in range(2):
                        p = jnp.exp2((scores[i, h, :, c * D : (c + 1) * D] - wide) * C2)
                        parts.append(p.astype(BF))
                probs.append(jnp.concatenate(parts, axis=1))
                tops.append(top)
            mixed = jnp.dot(
                jnp.concatenate(probs, axis=0), values, preferred_element_type=F32
            )
            here = g * (PER // 2) + k
            norms = lse_own[...]
            for e in range(2):
                row_sum = mixed[e * T : (e + 1) * T, D:]
                part = mixed[e * T : (e + 1) * T, :D] / row_sum
                obuf[here, :, e * D : (e + 1) * D] = part.astype(BF)
                norms = jnp.where(lane == 2 * here + e, tops[e] * SCALE + jnp.log(row_sum), norms)
            lse_own[...] = norms
            for d in range(1, N_KV):
                out_copy(here, d).start()
            out_ref[:, out_lanes(here)] = obuf[here, pl.ds(pl.multiple_of(z * 64, 64), 64), :]
            return 0

        lax.fori_loop(lo, hi, pair, 0)

    lse_own[...] = jnp.zeros((T, D), F32)
    stage_a(0)
    loads[2].wait()
    lax.fori_loop(0, PER, turn, 0)
    stage_b(0)
    stage_a(1)
    pass1_own(0)
    lax.fori_loop(PER, 2 * PER, turn, 0)
    stage_t(0, 2)
    stage_t(0, 1)
    stage_b(1)
    stage_t(0, 0)
    settle(0, 2)
    settle(0, 1)
    stage_a(2)
    pass1(0, 0, 2)
    stage_t(1, 2)
    stage_t(1, 1)
    settle(0, 0)
    stage_b(2)
    pass1(0, 2, 3)
    stage_t(1, 0)
    stage_a(3)
    pass1(0, 3, 4)
    for row in range(3):
        settle(1, row)
    pass2(0, 0, 1)
    for row in (2, 1, 0):
        stage_t(2, row)
    stage_b(3)
    pass2(0, 1, 4)
    for row in range(3):
        settle(2, row)
    pass1_own(1)
    pass1(1, 0, 1)
    for row in (2, 1, 0):
        stage_t(3, row)
    pass1(1, 1, 4)
    for row in range(3):
        settle(3, row)
    pass2(1, 0, 4)

    spread_rows = (
        lax.broadcasted_iota(jnp.int32, (T, N_TOK), 0) // 8
        == lax.broadcasted_iota(jnp.int32, (T, N_TOK), 1)
    ).astype(F32)
    plans = lax.dot_general(
        spread_rows.astype(BF), plan_ref[...].astype(F32).astype(BF),
        (((1,), (1,)), ((), ())), preferred_element_type=F32,
    )
    mine = lax.broadcasted_iota(jnp.int32, (T, N_TOK), 1) == j
    block = jnp.sum(jnp.where(mine, plans, 0.0), axis=1, keepdims=True).astype(jnp.int32)
    wanted = block * 8 + lax.broadcasted_iota(jnp.int32, (T, T), 0) % 8
    pick = (wanted == lax.broadcasted_iota(jnp.int32, (T, T), 1)).astype(F32).astype(BF)
    rest = lse_own[...]
    ordered = jnp.zeros((T, D), F32)
    for _ in range(3):
        piece = rest.astype(BF)
        rest = rest - piece.astype(F32)
        ordered = ordered + jnp.dot(pick, piece, preferred_element_type=F32)
    lse_send[...] = ordered.reshape(N_TOK, 8, D)
    lse_recv[j] = lse_send[j]

    def lse_copy(d):
        to = (j + d) % N_TOK
        return pltpu.make_async_remote_copy(
            src_ref=lse_send.at[to],
            dst_ref=lse_recv.at[j],
            send_sem=lsend.at[0],
            recv_sem=lrecv.at[0],
            device_id={"tok": to},
            device_id_type=MESH,
        )

    def lse_start(d, _):
        lse_copy(d).start()
        return 0

    def finish(part, sem):
        pltpu.make_async_copy(part, part, sem.at[0]).wait()

    lax.fori_loop(1, N_TOK, lse_start, 0)
    for t in range(4):
        drain(t)
    finish(lse_recv.at[pl.ds(0, N_TOK - 1)], lrecv)
    lse_ref[...] = lse_recv[...].reshape(T, D).T[:16, :]
    finish(lse_send.at[pl.ds(0, N_TOK - 1)], lsend)
    finish(obuf.at[pl.ds(0, 6)], osend)
    finish(out_ref.at[:, pl.ds(0, 48 * D)], orecv)


def body(queries, key_states, value_states, doc_lengths, block_plan):
    half = np.power(THETA, -(np.arange(D // 2) * 2.0 / D)).astype(np.float32)
    freq = jnp.asarray(np.concatenate([half, half])[None, :])
    vmem = pl.BlockSpec(memory_space=pltpu.VMEM)
    far = pl.BlockSpec(memory_space=pl.ANY)
    return pl.pallas_call(
        kernel,
        out_shape=(
            pltpu.VMEM((T // N_KV, N_KV * GROUPS * PER * D), BF),
            pltpu.VMEM((GROUPS * PER, T), F32),
        ),
        in_specs=[pl.BlockSpec(memory_space=pltpu.SMEM)] + [vmem] * 2 + [far] * 3,
        out_specs=(vmem, vmem),
        scratch_shapes=[
            pltpu.VMEM((T, GROUPS * PER * D), BF),
            pltpu.VMEM((T, GROUPS * D), BF),
            pltpu.VMEM((T, GROUPS * D), BF),
            pltpu.VMEM((4, SLOTS, T, D), BF),
            pltpu.VMEM((GROUPS * PER, T, D), BF),
            pltpu.VMEM((BACK + 1, PER, T, T), F32),
            pltpu.VMEM((PER, T, D), F32),
            pltpu.VMEM((GROUPS * PER // 2, T, 2 * D), BF),
            pltpu.VMEM((T, D), jnp.int32),
            pltpu.VMEM((T, D), F32),
            pltpu.VMEM((T, D), F32),
            pltpu.VMEM((T, D), F32),
            pltpu.VMEM((N_TOK, 8, D), F32),
            pltpu.VMEM((N_TOK, 8, D), F32),
            pltpu.SemaphoreType.DMA((3,)),
            pltpu.SemaphoreType.DMA((4,)),
            pltpu.SemaphoreType.DMA((4, SLOTS)),
            pltpu.SemaphoreType.DMA((4, 3)),
            pltpu.SemaphoreType.DMA((1,)),
            pltpu.SemaphoreType.DMA((1,)),
            pltpu.SemaphoreType.DMA((1,)),
            pltpu.SemaphoreType.DMA((1,)),
        ],
        compiler_params=pltpu.CompilerParams(
            collective_id=0, has_side_effects=True, vmem_limit_bytes=58 << 20
        ),
    )(doc_lengths, freq, block_plan, queries, key_states, value_states)


def solution(mesh):
    return jax.shard_map(
        body,
        mesh=mesh,
        in_specs=(P("tok", "kv"), P("tok", "kv"), P("tok", "kv"), P(), P()),
        out_specs=(P(("tok", "kv"), None), P("kv", "tok")),
        check_vma=False,
    )
```

```python
import functools
import math

import jax
import jax.numpy as jnp
import numpy as np
from jax import lax
from jax.experimental import pallas as pl
from jax.experimental.pallas import tpu as pltpu
from jax.sharding import PartitionSpec as P

D = 128
T = 256
GROUPS = 2
PER = 8
N_TOK = 32
N_KV = 4
DOCS = 16
BACK = 16
SLOTS = 24
NEG = -1e30
THETA = 500000.0
SCALE = 1.0 / math.sqrt(D)
C2 = SCALE * math.log2(math.e)
MESH = pl.DeviceIdType.MESH
BF = jnp.bfloat16
F32 = jnp.float32


def kernel(
    doc_ref, freq_ref, plan_ref, q_hbm, k_hbm, v_hbm,
    out_ref, lse_ref,
    q_ref, k_ref, v_ref, kv, qrot, scores, peak, obuf, start_ref, cos_ref, sin_ref, lse_own, lse_send, lse_recv,
    insem, ksend, krecv, trecv, osend, orecv, lsend, lrecv,
):
    j = lax.axis_index("tok")
    z = lax.axis_index("kv")
    core = j % 2
    x = (j // 2) % 4
    y = j // 8
    pos = j % 8
    own = core * 4 + x

    loads = [
        pltpu.make_async_copy(k_hbm, k_ref, insem.at[0]),
        pltpu.make_async_copy(v_hbm, v_ref, insem.at[1]),
        pltpu.make_async_copy(q_hbm, q_ref, insem.at[2]),
    ]
    for load in loads:
        load.start()

    def tok_of(y_, x_, core_):
        return ((y_ % 4) * 4 + (x_ % 4)) * 2 + core_

    barrier = pltpu.get_barrier_semaphore()

    def greet(d, _):
        pl.semaphore_signal(
            barrier, inc=1, device_id={"tok": (j + d) % N_TOK}, device_id_type=MESH
        )
        return 0

    lax.fori_loop(1, N_TOK, greet, 0)
    for d in range(1, N_KV):
        pl.semaphore_signal(
            barrier, inc=1, device_id={"kv": (z + d) % N_KV}, device_id_type=MESH
        )

    token = j * T + lax.broadcasted_iota(jnp.int32, (T, D), 0)
    lane = lax.broadcasted_iota(jnp.int32, (T, D), 1)
    start = jnp.zeros((T, D), jnp.int32)
    end = jnp.int32(0)
    for i in range(DOCS):
        end = end + doc_ref[i]
        start = jnp.where(token >= end, end, start)
    start_ref[...] = start - (j - BACK) * T
    angle = (token - start).astype(F32) * freq_ref[...]
    cos_ref[...] = jnp.cos(angle)
    sine = jnp.sin(angle)
    sin_ref[...] = jnp.where(lane < D // 2, -sine, sine)

    def rotate(block):
        wide = block.astype(F32)
        return (wide * cos_ref[...] + pltpu.roll(wide, D // 2, 1) * sin_ref[...]).astype(BF)

    loads[0].wait()
    loads[1].wait()
    for g in range(GROUPS):
        kv[2 * g, 16 + own] = rotate(k_ref[:, g * D : (g + 1) * D])
        kv[2 * g + 1, 16 + own] = v_ref[:, g * D : (g + 1) * D]

    pl.semaphore_wait(barrier, N_TOK - 1 + N_KV - 1)

    def copy(t, source, target, to):
        return pltpu.make_async_remote_copy(
            src_ref=kv.at[t, source],
            dst_ref=kv.at[t, target],
            send_sem=ksend.at[t],
            recv_sem=krecv.at[t, target],
            device_id={"tok": to},
            device_id_type=MESH,
        )

    def share(t, row):
        mine = pl.ds(row * 8 + core * 4, 4)
        return pltpu.make_async_remote_copy(
            src_ref=kv.at[t, mine],
            dst_ref=kv.at[t, mine],
            send_sem=ksend.at[t],
            recv_sem=trecv.at[t, row],
            device_id={"tok": tok_of(y, x, 1 - core)},
            device_id_type=MESH,
        )

    def needs(row, source_x, target_x):
        return (target_x > source_x) if row == 2 else (target_x < source_x)

    def spread(t, row):
        slot = row * 8 + own
        for d in (1, 3, 2):
            target_x = (x + d) % 4

            def send():
                copy(t, slot, slot, tok_of(y, target_x, core)).start()

            if row == 1:
                send()
            else:
                pl.when(needs(row, x, target_x))(send)

    def stage_a(t):
        for d in (1, 2):
            copy(t, 16 + own, 16 - 8 * d + own, tok_of(y + d, x, core)).start()
        spread(t, 2)

    def stage_b(t):
        for row in (1, 0):
            copy(t, 0, row * 8 + own, j).wait_recv()
            spread(t, row)

    def stage_t(t, row):
        for d in (1, 3, 2):
            source_x = (x + 4 - d) % 4

            def arrive():
                copy(t, 0, row * 8 + core * 4 + source_x, j).wait_recv()

            if row == 1:
                arrive()
            else:
                pl.when(needs(row, source_x, x))(arrive)
        share(t, row).start()

    def settle(t, row):
        pltpu.make_async_copy(
            kv.at[t, pl.ds(0, 4)], kv.at[t, pl.ds(row * 8, 4)], trecv.at[t, row]
        ).wait()

    def drain(t):
        part = kv.at[t, pl.ds(0, 20)]
        pltpu.make_async_copy(part, part, ksend.at[t]).wait()

    def turn(h, _):
        lanes = pl.ds(pl.multiple_of(h * D, D), D)
        qrot[h] = rotate(q_ref[:, lanes])
        return 0

    def tile(t, i):
        at = pos + i
        place = at % 8
        return kv[t, (at // 8) * 8 + (place % 2) * 4 + place // 2]

    column = lax.broadcasted_iota(jnp.int32, (8, D), 1)

    def score(g, h, keys):
        return lax.dot_general(
            qrot[g * PER + h], keys, (((1,), (1,)), ((), ())), preferred_element_type=F32
        )

    def pass1(g, lo, hi):
        def pair(k, _):
            i = BACK // 4 - 1 - k
            keys = jnp.concatenate([tile(2 * g, 4 * i + e) for e in range(4)], axis=0)

            def head(h, _):
                s = score(g, h, keys)
                best = peak[h]
                for c in range(8):
                    index = column + (i * 1024 + c * D)
                    allowed = index[None] >= start_ref[...].reshape(T // 8, 8, D)
                    part = jnp.where(allowed.reshape(T, D), s[:, c * D : (c + 1) * D], NEG)
                    scores[i * 4 + c // 2, h, :, (c % 2) * D : (c % 2 + 1) * D] = part
                    best = jnp.maximum(best, part)
                peak[h] = best
                return 0

            lax.fori_loop(0, PER, head, 0, unroll=True)
            return 0

        lax.fori_loop(lo, hi, pair, 0)

    def pass1_own(g):
        keys = tile(2 * g, BACK)

        def diagonal(h, _):
            s = score(g, h, keys)
            row = lax.broadcasted_iota(jnp.int32, (T, D), 0)
            best = jnp.full((T, D), NEG, F32)
            for c in range(2):
                index = lax.broadcasted_iota(jnp.int32, (T, D), 1) + c * D
                allowed = (index + BACK * T >= start_ref[...]) & (index <= row)
                part = jnp.where(allowed, s[:, c * D : (c + 1) * D], NEG)
                scores[BACK, h, :, c * D : (c + 1) * D] = part
                best = jnp.maximum(best, part)
            peak[h] = best
            return 0

        lax.fori_loop(0, PER, diagonal, 0, unroll=True)

    def out_lanes(two):
        return pl.ds(pl.multiple_of((z * 8 + two) * 2 * D, 2 * D), 2 * D)

    def out_copy(two, d):
        to = (z + d) % N_KV
        return pltpu.make_async_remote_copy(
            src_ref=obuf.at[two, pl.ds(to * 64, 64), :],
            dst_ref=out_ref.at[:, out_lanes(two)],
            send_sem=osend.at[0],
            recv_sem=orecv.at[0],
            device_id={"kv": to},
            device_id_type=MESH,
        )

    def pass2(g, lo, hi):
        values = jnp.concatenate([tile(2 * g + 1, i) for i in range(BACK + 1)], axis=0)
        values = jnp.concatenate([values, jnp.ones_like(values)], axis=1)

        def pair(k, _):
            probs, tops = [], []
            for e in range(2):
                h = 2 * k + e
                top = jnp.max(peak[h], axis=1, keepdims=True)
                wide = jnp.broadcast_to(top, (T, D))
                parts = []
                for i in range(BACK + 1):
                    for c in range(2):
                        p = jnp.exp2((scores[i, h, :, c * D : (c + 1) * D] - wide) * C2)
                        parts.append(p.astype(BF))
                probs.append(jnp.concatenate(parts, axis=1))
                tops.append(top)
            mixed = jnp.dot(
                jnp.concatenate(probs, axis=0), values, preferred_element_type=F32
            )
            here = g * (PER // 2) + k
            norms = lse_own[...]
            for e in range(2):
                row_sum = mixed[e * T : (e + 1) * T, D:]
                part = mixed[e * T : (e + 1) * T, :D] / row_sum
                obuf[here, :, e * D : (e + 1) * D] = part.astype(BF)
                norms = jnp.where(lane == 2 * here + e, tops[e] * SCALE + jnp.log(row_sum), norms)
            lse_own[...] = norms
            for d in range(1, N_KV):
                out_copy(here, d).start()
            out_ref[:, out_lanes(here)] = obuf[here, pl.ds(pl.multiple_of(z * 64, 64), 64), :]
            return 0

        lax.fori_loop(lo, hi, pair, 0)

    lse_own[...] = jnp.zeros((T, D), F32)
    stage_a(0)
    loads[2].wait()
    lax.fori_loop(0, PER, turn, 0)
    stage_b(0)
    stage_a(1)
    lax.fori_loop(PER, 2 * PER, turn, 0)
    stage_t(0, 2)
    pass1_own(0)
    stage_t(0, 1)
    stage_b(1)
    stage_t(0, 0)
    settle(0, 2)
    settle(0, 1)
    stage_a(2)
    pass1(0, 0, 2)
    stage_t(1, 2)
    stage_t(1, 1)
    settle(0, 0)
    stage_b(2)
    pass1(0, 2, 3)
    stage_t(1, 0)
    stage_a(3)
    pass1(0, 3, 4)
    for row in range(3):
        settle(1, row)
    pass2(0, 0, 1)
    for row in (2, 1, 0):
        stage_t(2, row)
    stage_b(3)
    pass2(0, 1, 4)
    for row in range(3):
        settle(2, row)
    pass1_own(1)
    pass1(1, 0, 1)
    for row in (2, 1, 0):
        stage_t(3, row)
    pass1(1, 1, 4)
    for row in range(3):
        settle(3, row)
    pass2(1, 0, 4)

    spread_rows = (
        lax.broadcasted_iota(jnp.int32, (T, N_TOK), 0) // 8
        == lax.broadcasted_iota(jnp.int32, (T, N_TOK), 1)
    ).astype(F32)
    plans = lax.dot_general(
        spread_rows.astype(BF), plan_ref[...].astype(F32).astype(BF),
        (((1,), (1,)), ((), ())), preferred_element_type=F32,
    )
    mine = lax.broadcasted_iota(jnp.int32, (T, N_TOK), 1) == j
    block = jnp.sum(jnp.where(mine, plans, 0.0), axis=1, keepdims=True).astype(jnp.int32)
    wanted = block * 8 + lax.broadcasted_iota(jnp.int32, (T, T), 0) % 8
    pick = (wanted == lax.broadcasted_iota(jnp.int32, (T, T), 1)).astype(F32).astype(BF)
    rest = lse_own[...]
    ordered = jnp.zeros((T, D), F32)
    for _ in range(3):
        piece = rest.astype(BF)
        rest = rest - piece.astype(F32)
        ordered = ordered + jnp.dot(pick, piece, preferred_element_type=F32)
    lse_send[...] = ordered.reshape(N_TOK, 8, D)
    lse_recv[j] = lse_send[j]

    def lse_copy(d):
        to = (j + d) % N_TOK
        return pltpu.make_async_remote_copy(
            src_ref=lse_send.at[to],
            dst_ref=lse_recv.at[j],
            send_sem=lsend.at[0],
            recv_sem=lrecv.at[0],
            device_id={"tok": to},
            device_id_type=MESH,
        )

    def lse_start(d, _):
        lse_copy(d).start()
        return 0

    def finish(part, sem):
        pltpu.make_async_copy(part, part, sem.at[0]).wait()

    lax.fori_loop(1, N_TOK, lse_start, 0)
    for t in range(4):
        drain(t)
    finish(lse_recv.at[pl.ds(0, N_TOK - 1)], lrecv)
    lse_ref[...] = lse_recv[...].reshape(T, D).T[:16, :]
    finish(lse_send.at[pl.ds(0, N_TOK - 1)], lsend)
    finish(obuf.at[pl.ds(0, 6)], osend)
    finish(out_ref.at[:, pl.ds(0, 48 * D)], orecv)


def body(queries, key_states, value_states, doc_lengths, block_plan):
    half = np.power(THETA, -(np.arange(D // 2) * 2.0 / D)).astype(np.float32)
    freq = jnp.asarray(np.concatenate([half, half])[None, :])
    vmem = pl.BlockSpec(memory_space=pltpu.VMEM)
    far = pl.BlockSpec(memory_space=pl.ANY)
    return pl.pallas_call(
        kernel,
        out_shape=(
            pltpu.VMEM((T // N_KV, N_KV * GROUPS * PER * D), BF),
            pltpu.VMEM((GROUPS * PER, T), F32),
        ),
        in_specs=[pl.BlockSpec(memory_space=pltpu.SMEM)] + [vmem] * 2 + [far] * 3,
        out_specs=(vmem, vmem),
        scratch_shapes=[
            pltpu.VMEM((T, GROUPS * PER * D), BF),
            pltpu.VMEM((T, GROUPS * D), BF),
            pltpu.VMEM((T, GROUPS * D), BF),
            pltpu.VMEM((4, SLOTS, T, D), BF),
            pltpu.VMEM((GROUPS * PER, T, D), BF),
            pltpu.VMEM((BACK + 1, PER, T, T), F32),
            pltpu.VMEM((PER, T, D), F32),
            pltpu.VMEM((GROUPS * PER // 2, T, 2 * D), BF),
            pltpu.VMEM((T, D), jnp.int32),
            pltpu.VMEM((T, D), F32),
            pltpu.VMEM((T, D), F32),
            pltpu.VMEM((T, D), F32),
            pltpu.VMEM((N_TOK, 8, D), F32),
            pltpu.VMEM((N_TOK, 8, D), F32),
            pltpu.SemaphoreType.DMA((3,)),
            pltpu.SemaphoreType.DMA((4,)),
            pltpu.SemaphoreType.DMA((4, SLOTS)),
            pltpu.SemaphoreType.DMA((4, 3)),
            pltpu.SemaphoreType.DMA((1,)),
            pltpu.SemaphoreType.DMA((1,)),
            pltpu.SemaphoreType.DMA((1,)),
            pltpu.SemaphoreType.DMA((1,)),
        ],
        compiler_params=pltpu.CompilerParams(
            collective_id=0, has_side_effects=True, vmem_limit_bytes=58 << 20
        ),
    )(doc_lengths, freq, block_plan, queries, key_states, value_states)


def solution(mesh):
    return jax.shard_map(
        body,
        mesh=mesh,
        in_specs=(P("tok", "kv"), P("tok", "kv"), P("tok", "kv"), P(), P()),
        out_specs=(P(("tok", "kv"), None), P("kv", "tok")),
        check_vma=False,
    )
```
